512 devices in a mesh: seq: 128 (over y, z, core), head: 4 (over x).
Axes of the slice: x: 4, y: 8, z: 8, core: 2. Of those that a mesh axis runs over, the one named last changes fastest.
Arguments:
- queries: bfloat16 [32768, 2048], P('seq', 'head'), may hold values from -6 to 6
- key_rows: bfloat16 [32768, 2048], P('seq', 'head'), may hold values from -6 to 6
- value_rows: bfloat16 [32768, 2048], P('seq', 'head'), may hold values from -6 to 6
- out_gain: float32 [2048], P('head'), may hold values from 0.5 to 1.5
- doc_starts: int32 [1024], P('seq'), may hold values from 0 to 256, as said below
- doc_domains: int32 [1024], P('seq'), may hold values from 0 to 7
- domain_weights: int32 [8], replicated, may hold values from 1 to 8, as said below
- cotangent: bfloat16 [32768, 2048], P('seq', 'head'), may hold values from -0.3125 to 0.3125
- weight: float32 [2048, 2048], P('head', 'seq'), may hold values from -1.5 to 1.5
- moment_first: float32 [2048, 2048], P('head', 'seq'), may hold values from -6 to 6
- moment_second: float32 [2048, 2048], P('head', 'seq'), may hold values from 0.5 to 8
Outputs:
- attention: bfloat16 [32768, 2048], P('seq', 'head')
- new_weight: float32 [2048, 2048], P('head', 'seq')
- new_first: float32 [2048, 2048], P('head', 'seq')
- new_second: float32 [2048, 2048], P('head', 'seq')
The draws below stay inside these ranges and needn't reach their ends.
Inputs may be any that keep to these rules, and one draw needn't show every extreme that they name: `doc_starts`: each block's 8 entries are ascending; entries below 256 are distinct start offsets and come first, entries equal to 256 mark unused slots. Some block uses all slots and has a start at offset 0, some block has no start, and most blocks have none. `domain_weights`: each of 1 to 8 once.
All inputs are finite; a program needn't handle non-finite values.
Results may differ from the reference program's by a relative error of at most 0.0049.
Values may be sent and summed in bfloat16 or wider, within the bound.
No kernel may reach another device: no remote copies, remote signals or barrier semaphores. Data moves between devices by JAX's collectives and lax.ppermute only.
A program may use at most 128 MiB of HBM per device.

```python
import math
import jax
import jax.numpy as jnp
from jax import lax

D = 2048
HEADS = 16
HEAD_DIM = 128
TOK_DEV = 256
DOCS_DEV = 8
DOMAINS = 8
TOKENS = 32768


def pick_full(key):
    shard_count = TOKENS // TOK_DEV
    return jax.random.randint(jax.random.fold_in(key, 7), (), 0, max(shard_count // 4, 1)).astype(jnp.int32)


def start_counts(key):
    shard_count = TOKENS // TOK_DEV
    key_busy = jax.random.fold_in(key, 11)
    key_count = jax.random.fold_in(key, 13)
    full_device = pick_full(key)
    device_ids = jnp.arange(shard_count, dtype=jnp.int32)
    busy_device = jax.random.randint(key_busy, (shard_count,), 0, 2) == 0
    counts = jax.random.randint(key_count, (shard_count,), 1, DOCS_DEV + 1)
    counts = jnp.where(busy_device & (device_ids < full_device), counts, 0)
    counts = jnp.where(device_ids == full_device, DOCS_DEV, counts)
    return (counts.astype(jnp.int32), full_device)


def draw_doc_starts(key, part):
    shard_count = TOKENS // TOK_DEV
    counts, full_device = start_counts(key)
    key_perm = jax.random.fold_in(key, 17)

    def take_slots(subkey):
        return jax.random.permutation(subkey, TOK_DEV)[:DOCS_DEV]
    permuted = jax.vmap(take_slots)(jax.random.split(key_perm, shard_count)).astype(jnp.int32)
    slot_ids = jnp.arange(DOCS_DEV, dtype=jnp.int32)
    offsets = jnp.where(slot_ids[None, :] < counts[:, None], permuted, TOK_DEV)
    offsets = jnp.sort(offsets, axis=1)
    offsets = offsets.at[full_device, 0].set(0)
    return offsets.reshape(-1).astype(jnp.int32)


def draw_doc_domains(key, part):
    shard_count = TOKENS // TOK_DEV
    full_device = pick_full(key)
    drawn = jax.random.randint(jax.random.fold_in(key, 19), (shard_count, DOCS_DEV), 0, DOMAINS)
    nonzero = jax.random.randint(jax.random.fold_in(key, 23), (), 1, DOMAINS)
    drawn = drawn.at[full_device, DOCS_DEV - 1].set(nonzero)
    return drawn.reshape(-1).astype(jnp.int32)


def draw_domain_weights(key, part):
    return (jax.random.permutation(jax.random.fold_in(key, 29), DOMAINS) + 1).astype(jnp.int32)


def strengthened(drawn, own_key, source, target, blocks, factor):
    def block_of(dim):
        return (jnp.arange(drawn.shape[dim]) // (drawn.shape[dim] // blocks)).reshape((-1,) + (1,) * (drawn.ndim - 1 - dim))

    first = jax.random.permutation(own_key, blocks)[block_of(target)]
    second = (block_of(target) + blocks // 2) % blocks
    return jnp.where((block_of(source) == first) | (block_of(source) == second), factor * drawn, drawn)


def steps_of(rng, extent, cuts, least, high):
    gain = 1.0
    for axis_at, parts in cuts:
        heights = jax.random.uniform(jax.random.fold_in(jax.random.fold_in(rng, 6), axis_at), (parts,), jnp.float32, least / len(cuts), high / len(cuts))
        gain = gain * jnp.repeat(jnp.exp(heights), extent[axis_at] // parts).reshape((-1,) + (1,) * (len(extent) - 1 - axis_at))
    return gain


def scatter_about(rng, extent, width, most, cuts=(), kind=jnp.bfloat16):
    entries = jax.random.normal(rng, extent, jnp.float32) * width
    if len(cuts) > 0:
        entries = steps_of(rng, extent, cuts, -0.22, 0.18) * entries
    return jnp.clip(entries, min=-most, max=most).astype(kind)


def noise_with(own_key, extent, spread, most, cuts, heavy, kind=jnp.bfloat16):
    array = spread * jax.random.normal(own_key, extent, jnp.float32)
    if cuts:
        array = array * steps_of(own_key, extent, cuts, -0.22, 0.18)
    return jnp.clip(strengthened(array, jax.random.fold_in(own_key, 3), *heavy), -most, most).astype(kind)


def setup_inputs(seed: int = 0) -> dict:
    arg_keys = jax.random.split(jax.random.key(seed), 12)
    return {
        "queries": scatter_about(arg_keys[0], (TOKENS, HEADS * HEAD_DIM), 1.0, 6.0, ((0, 128), (1, 4))),
        "key_rows": scatter_about(arg_keys[1], (TOKENS, HEADS * HEAD_DIM), 1.0, 6.0, ((0, 128), (1, 4))),
        "value_rows": scatter_about(arg_keys[2], (TOKENS, HEADS * HEAD_DIM), 1.0, 6.0, ((0, 128), (1, 4))),
        "out_gain": jnp.clip(1.0 + 0.1 * jax.random.normal(arg_keys[3], (HEADS * HEAD_DIM,), jnp.float32), 0.5, 1.5),
        "doc_starts": draw_doc_starts(jax.random.fold_in(arg_keys[11], 71), 0),
        "doc_domains": draw_doc_domains(jax.random.fold_in(arg_keys[11], 71), 0),
        "domain_weights": draw_domain_weights(jax.random.fold_in(arg_keys[11], 71), 0),
        "cotangent": noise_with(arg_keys[7], (TOKENS, D), (TOKENS ** -0.5), 0.3125, ((0, 128), (1, 4)), (0, 1, 128, 5.5)),
        "weight": scatter_about(arg_keys[8], (HEADS * HEAD_DIM, D), 0.1, 1.5, ((0, 4), (1, 128)), jnp.float32),
        "moment_first": scatter_about(arg_keys[9], (HEADS * HEAD_DIM, D), 1.0, 6.0, ((0, 4), (1, 128)), jnp.float32),
        "moment_second": jnp.clip(jnp.exp(math.log(8.0) - 2.7725887 * jax.random.uniform(arg_keys[10], (HEADS * HEAD_DIM, D), jnp.float32) ** steps_of(arg_keys[10], (HEADS * HEAD_DIM, D), ((0, 4), (1, 128)), -0.2, 0.2)), 0.5, 8.0),
    }


first_debias = 0.9999734386011124
second_debias = 0.994079470779666

def local_docs(starts, row_count):
    positions = lax.broadcasted_iota(jnp.int32, (row_count, starts.shape[0]), 0)
    return lax.optimization_barrier(jnp.sum((starts[None, :] <= positions).astype(jnp.int32), axis=1))

def shard_attention(queries, key_rows, value_rows, doc_local, carried, gain_vec, head_count):
    row_count = queries.shape[0]
    head_width = queries.shape[1] // head_count
    query_heads = queries.reshape(row_count, head_count, head_width).astype(jnp.float32)
    key_heads = key_rows.reshape(row_count, head_count, head_width).astype(jnp.float32)
    value_heads = value_rows.reshape(row_count, head_count, head_width).astype(jnp.float32)
    carried_half = carried.astype(jnp.bfloat16).astype(jnp.float32)
    block_rows = 512 if row_count % 512 == 0 else row_count
    pieces = []
    for row_start in range(0, row_count, block_rows):
        row_end = row_start + block_rows
        query_block = query_heads[row_start:row_end]
        scores = jnp.einsum('thd,shd->hts', query_block, key_heads[:row_end])
        row_pos = lax.broadcasted_iota(jnp.int32, (block_rows, row_end), 0) + row_start
        col_pos = lax.broadcasted_iota(jnp.int32, (block_rows, row_end), 1)
        visible = (col_pos <= row_pos) & (doc_local[row_start:row_end][:, None] == doc_local[None, :row_end])
        weights_half = jnp.where(visible[None], scores, 0.0).astype(jnp.bfloat16).astype(jnp.float32)
        inner_part = jnp.einsum('hts,shd->thd', weights_half, value_heads[:row_end])
        carried_part = jnp.einsum('thd,hde->the', query_block, carried_half)
        raw_sum = inner_part + jnp.where((doc_local[row_start:row_end] == 0)[:, None, None], carried_part, 0.0)
        inv_scale = lax.rsqrt(lax.optimization_barrier(jnp.mean(raw_sum * raw_sum, axis=2, keepdims=True)) + 1e-05)
        normed = raw_sum * inv_scale * gain_vec.reshape(1, head_count, head_width)
        pieces.append(normed.astype(jnp.bfloat16).reshape(block_rows, head_count * head_width))
    return jnp.concatenate(pieces, axis=0)

def reference(queries, key_rows, value_rows, out_gain, doc_starts, doc_domains, domain_weights, cotangent, weight, moment_first, moment_second):
    shard_count = TOKENS // TOK_DEV
    width_all = HEADS * HEAD_DIM
    query_sh = queries.reshape(shard_count, TOK_DEV, width_all)
    key_sh = key_rows.reshape(shard_count, TOK_DEV, width_all)
    value_sh = value_rows.reshape(shard_count, TOK_DEV, width_all)
    starts_sh = doc_starts.reshape(shard_count, DOCS_DEV)
    domains_sh = doc_domains.reshape(shard_count, DOCS_DEV)

    def advance(carry, inputs):
        carried, domain_in = carry
        query_block, key_block, value_block, starts, domains = inputs
        doc_local = local_docs(starts, TOK_DEV)
        started = jnp.sum((starts < TOK_DEV).astype(jnp.int32))
        slot_ids = lax.broadcasted_iota(jnp.int32, (DOCS_DEV,), 0)
        last_domain = jnp.sum(jnp.where(slot_ids == started - 1, domains, 0))
        attention = shard_attention(query_block, key_block, value_block, doc_local, carried, out_gain, HEADS)
        key_heads = key_block.reshape(TOK_DEV, HEADS, HEAD_DIM).astype(jnp.float32)
        value_heads = value_block.reshape(TOK_DEV, HEADS, HEAD_DIM).astype(jnp.float32)
        tail_keys = jnp.where((doc_local == started)[:, None, None], key_heads, 0.0)
        own_state = jnp.einsum('thd,the->hde', tail_keys, value_heads)
        token_domain = jnp.where(doc_local == 0, domain_in, lax.optimization_barrier(jnp.sum(jnp.where(doc_local[:, None] - 1 == slot_ids[None, :], domains[None, :], 0), axis=1))).astype(jnp.int32)
        new_carried = jnp.where(started > 0, own_state, carried + own_state)
        new_domain = jnp.where(started > 0, last_domain, domain_in).astype(jnp.int32)
        return ((new_carried, new_domain), (attention, token_domain))
    init = (jnp.zeros((HEADS, HEAD_DIM, HEAD_DIM), jnp.float32), jnp.zeros((), jnp.int32))
    final_carry, outputs = lax.scan(advance, init, (query_sh, key_sh, value_sh, starts_sh, domains_sh))
    attention = outputs[0].reshape(TOKENS, width_all)
    token_domain = outputs[1].reshape(TOKENS)
    domain_ids = lax.broadcasted_iota(jnp.int32, (TOKENS, DOMAINS), 1)
    token_weight = lax.optimization_barrier(jnp.sum(jnp.where(token_domain[:, None] == domain_ids, domain_weights[None, :], 0), axis=1)).astype(jnp.float32)
    weighted = (cotangent.astype(jnp.float32) * token_weight[:, None]).astype(jnp.bfloat16)
    gradient = jnp.dot(attention.T, weighted, preferred_element_type=jnp.float32)
    new_first = 0.9 * moment_first + 0.1 * gradient
    new_second = 0.95 * moment_second + 0.05 * gradient * gradient
    corrected_first = new_first / first_debias
    corrected_second = new_second / second_debias
    new_weight = weight - 0.01 * (corrected_first / (jnp.sqrt(corrected_second) + 1e-08) + 0.1 * weight)
    return (attention, new_weight, new_first, new_second)
```

```python
import jax
import jax.numpy as jnp
from jax import lax
from jax.experimental import pallas as pl
from jax.experimental.pallas import tpu as pltpu
from jax.sharding import Mesh, PartitionSpec as P

HEAD_DIM = 128
LANES = 128

first_debias = 0.9999734386011124
second_debias = 0.994079470779666

f32, bf16, i32 = jnp.float32, jnp.bfloat16, jnp.int32
VMEM_SPEC = pl.BlockSpec(memory_space=pltpu.VMEM)
SMEM_SPEC = pl.BlockSpec(memory_space=pltpu.SMEM)


def iota(shape, dim):
    return lax.broadcasted_iota(i32, shape, dim)


def docs_along(starts_ref, shape, dim):
    positions = iota(shape, dim)
    total = jnp.zeros(shape, i32)
    for slot in range(starts_ref.shape[0]):
        total = total + (starts_ref[slot] <= positions).astype(i32)
    return total


def started_and_domain(starts_ref, domains_ref, row_count):
    slots = starts_ref.shape[0]
    started = jnp.int32(0)
    for slot in range(slots):
        started = started + (starts_ref[slot] < row_count).astype(i32)
    last_domain = jnp.int32(0)
    for slot in range(slots):
        last_domain = last_domain + jnp.where(slot == started - 1, domains_ref[slot], 0)
    return started, last_domain


def dot(a, b, contract):
    return lax.dot_general(a, b, (contract, ((), ())), preferred_element_type=f32)


def state_kernel(key_ref, value_ref, starts_ref, domains_ref, out_ref):
    row_count, width = key_ref.shape
    started, last_domain = started_and_domain(starts_ref, domains_ref, row_count)
    in_tail = docs_along(starts_ref, (row_count, HEAD_DIM), 0) == started
    for head in range(width // HEAD_DIM):
        cols = slice(head * HEAD_DIM, (head + 1) * HEAD_DIM)
        keys = jnp.where(in_tail, key_ref[:, cols].astype(f32), 0.0).astype(bf16)
        out_ref[:, cols] = dot(keys, value_ref[:, cols], ((0,), (0,)))
    lane = iota((HEAD_DIM, LANES), 1)
    flag = (started > 0).astype(f32)
    out_ref[:, width:] = jnp.where(
        lane == 0, flag, jnp.where(lane == 1, last_domain.astype(f32), 0.0)
    )


def carry_kernel(own_ref, states_ref, carried_ref, domain_ref, *, width, rows):
    blocks = states_ref.shape[0]
    stride = width + LANES
    info = states_ref[:, width : width + LANES]
    flag_col = info[:, 0:1]
    domain_col = info[:, 1:2]
    here = iota((blocks, blocks), 0)
    there = iota((blocks, blocks), 1)
    flag_row = jnp.sum(jnp.where(here == there, flag_col, 0.0), axis=0, keepdims=True)
    latest = jnp.max(
        jnp.where((flag_row > 0.0) & (there < here), there, -1), axis=1, keepdims=True
    )
    joined = jnp.where((there < here) & (there >= latest), 1.0, 0.0).astype(bf16)
    for row in range(rows):
        state = states_ref[:, row * stride : row * stride + width]
        high = state.astype(bf16)
        rest = state - high.astype(f32)
        middle = rest.astype(bf16)
        low = (rest - middle.astype(f32)).astype(bf16)
        total = dot(joined, high, ((1,), (0,)))
        total = total + dot(joined, middle, ((1,), (0,)))
        total = total + dot(joined, low, ((1,), (0,)))
        carried_ref[:, row * width : (row + 1) * width] = total.astype(bf16)
    block_ids = iota((blocks, 1), 0)
    before = (flag_col > 0.0) & (block_ids < own_ref[0])
    last_block = jnp.max(jnp.where(before, block_ids, -1))
    domain_ref[0] = jnp.sum(jnp.where(block_ids == last_block, domain_col, 0.0)).astype(i32)


def inner_kernel(query_ref, key_ref, value_ref, starts_ref, out_ref):
    row_count, width = query_ref.shape
    square = (row_count, row_count)
    visible = (iota(square, 1) <= iota(square, 0)) & (
        docs_along(starts_ref, square, 0) == docs_along(starts_ref, square, 1)
    )
    for head in range(width // HEAD_DIM):
        cols = slice(head * HEAD_DIM, (head + 1) * HEAD_DIM)
        scores = dot(query_ref[:, cols], key_ref[:, cols], ((1,), (1,)))
        scores = jnp.where(visible, scores, 0.0).astype(bf16)
        out_ref[:, cols] = dot(scores, value_ref[:, cols], ((1,), (0,)))


def attention_kernel(
    query_ref, inner_ref, carried_ref, gain_ref, starts_ref, domains_ref, weights_ref,
    domain_in_ref, out_ref, shared_ref,
):
    row_count, width = query_ref.shape
    first_doc = docs_along(starts_ref, (row_count, HEAD_DIM), 0) == 0
    for head in range(width // HEAD_DIM):
        cols = slice(head * HEAD_DIM, (head + 1) * HEAD_DIM)
        part = dot(query_ref[:, cols], carried_ref[:, cols], ((1,), (0,)))
        raw = inner_ref[:, cols] + jnp.where(first_doc, part, 0.0)
        scale = lax.rsqrt(jnp.mean(raw * raw, axis=1, keepdims=True) + 1e-05)
        normed = (raw * scale * gain_ref[:, cols]).astype(bf16)
        out_ref[:, cols] = normed
        shared_ref[:row_count, cols] = normed
    doc = docs_along(starts_ref, (16, row_count), 1)
    domain = jnp.where(doc == 0, domain_in_ref[0], 0)
    for slot in range(starts_ref.shape[0]):
        domain = jnp.where(doc == slot + 1, domains_ref[slot], domain)
    weight = jnp.zeros((16, row_count), f32)
    for which in range(weights_ref.shape[0]):
        weight = jnp.where(domain == which, weights_ref[which].astype(f32), weight)
    shared_ref[row_count:, :row_count] = weight.astype(bf16)
    shared_ref[row_count:, row_count:] = jnp.zeros((16, width - row_count), bf16)


def turn_kernel(cotangent_ref, out_ref, *, owned):
    width = cotangent_ref.shape[1]
    turned = cotangent_ref[...].T
    for core in range(2):
        for pair in range(width // (2 * owned)):
            piece = turned[(2 * pair + core) * owned : (2 * pair + core + 1) * owned]
            for group in range(out_ref.shape[1]):
                out_ref[core, group, pair * owned : (pair + 1) * owned] = piece


def gradient_kernel(shared_ref, cotangent_ref, out_ref):
    cores, groups, cols, row_count = cotangent_ref.shape
    for group in range(groups):
        total = None
        for core in range(cores):
            weight = shared_ref[core, row_count : row_count + 1, :row_count].astype(f32)
            weighted = (cotangent_ref[core, group].astype(f32) * weight).astype(bf16)
            part = dot(weighted, shared_ref[core, :row_count, :], ((1,), (0,)))
            total = part if total is None else total + part
        out_ref[group * cols : (group + 1) * cols] = total.astype(bf16)


def update_kernel(
    parts_ref, weight_ref, first_ref, second_ref, new_weight_ref, new_first_ref, new_second_ref
):
    gradient = jnp.sum(parts_ref[...].astype(f32), axis=0)
    weight = weight_ref[...]
    new_first = 0.9 * first_ref[...] + 0.1 * gradient
    new_second = 0.95 * second_ref[...] + 0.05 * gradient * gradient
    corrected_first = new_first / first_debias
    corrected_second = new_second / second_debias
    new_first_ref[...] = new_first
    new_second_ref[...] = new_second
    new_weight_ref[...] = weight - 0.01 * (
        corrected_first / (jnp.sqrt(corrected_second) + 1e-08) + 0.1 * weight
    )


def shape(dims, dtype):
    return jax.ShapeDtypeStruct(dims, dtype)


def on_device(
    queries, key_rows, value_rows, out_gain, doc_starts, doc_domains, domain_weights,
    cotangent, weight, moment_first, moment_second,
):
    chips, groups = lax.axis_size("chip"), lax.axis_size("group")
    blocks = 2 * chips
    row_count, width = queries.shape
    owned = weight.shape[1]
    rows = HEAD_DIM // blocks
    own_block = (lax.axis_index("chip") * 2 + lax.axis_index("core")).reshape(1).astype(i32)
    V, S = VMEM_SPEC, SMEM_SPEC

    turned = pl.pallas_call(
        lambda c, o: turn_kernel(c, o, owned=owned),
        out_shape=shape((2, groups, width // 2, row_count), bf16),
        in_specs=[V], out_specs=V, name="turn",
    )(cotangent)
    states = pl.pallas_call(
        state_kernel,
        out_shape=shape((HEAD_DIM, width + LANES), f32),
        in_specs=[V, V, S, S], out_specs=V, name="state",
    )(key_rows, value_rows, doc_starts, doc_domains)
    states = states.reshape(blocks, rows * (width + LANES))
    states = lax.all_to_all(states, ("chip", "core"), 0, 0, tiled=True)
    turned = turned.reshape(2 * groups, width // 2, row_count)
    turned = lax.all_to_all(turned, ("core", "group"), 0, 0, tiled=True)
    turned = turned.reshape(2, groups, width // 2, row_count)
    inner = pl.pallas_call(
        inner_kernel,
        out_shape=shape((row_count, width), f32),
        in_specs=[V, V, V, S], out_specs=V, name="inner",
    )(queries, key_rows, value_rows, doc_starts)
    carried, domain_in = pl.pallas_call(
        lambda *refs: carry_kernel(*refs, width=width, rows=rows),
        out_shape=(shape((blocks, rows * width), bf16), shape((1,), i32)),
        in_specs=[S, V], out_specs=(V, S), name="carry",
    )(own_block, states)
    carried = lax.all_to_all(carried, ("chip", "core"), 0, 0, tiled=True)
    attention, shared = pl.pallas_call(
        attention_kernel,
        out_shape=(shape((row_count, width), bf16), shape((row_count + 16, width), bf16)),
        in_specs=[V, V, V, V, S, S, S, S], out_specs=(V, V), name="attention",
    )(
        queries, inner, carried.reshape(HEAD_DIM, width), out_gain.reshape(1, width),
        doc_starts, doc_domains, domain_weights, domain_in,
    )
    shared = lax.all_gather(shared, "core", axis=0, tiled=False)
    partial = pl.pallas_call(
        gradient_kernel,
        out_shape=shape((groups * width // 2, width), bf16),
        in_specs=[V, V], out_specs=V, name="gradient",
    )(shared, turned)
    partial = partial.reshape(chips, owned, width)
    partial = lax.all_to_all(partial, "chip", 0, 0, tiled=True)
    new_weight, new_first, new_second = pl.pallas_call(
        update_kernel,
        out_shape=(shape((owned, width), f32),) * 3,
        in_specs=[V] * 4, out_specs=(V,) * 3, name="update",
    )(partial, weight.T, moment_first.T, moment_second.T)
    return (attention, new_weight.T, new_first.T, new_second.T)


def solution(mesh):
    blocks, groups = mesh.devices.shape
    split = Mesh(mesh.devices.reshape(blocks // 2, 2, groups), ("chip", "core", "group"))
    seq, head = ("chip", "core"), "group"
    in_specs = (
        P(seq, head), P(seq, head), P(seq, head), P(head), P(seq), P(seq), P(),
        P(seq, head), P(head, seq), P(head, seq), P(head, seq),
    )
    out_specs = (P(seq, head), P(head, seq), P(head, seq), P(head, seq))
    return jax.shard_map(
        on_device, mesh=split, in_specs=in_specs, out_specs=out_specs, check_vma=False
    )
```

```python
import jax
import jax.numpy as jnp
from jax import lax
from jax.experimental import pallas as pl
from jax.experimental.pallas import tpu as pltpu
from jax.sharding import Mesh, PartitionSpec as P

HEAD_DIM = 128
LANES = 128

first_debias = 0.9999734386011124
second_debias = 0.994079470779666

f32, bf16, i32 = jnp.float32, jnp.bfloat16, jnp.int32
VMEM_SPEC = pl.BlockSpec(memory_space=pltpu.VMEM)
SMALL = pltpu.CompilerParams(vmem_limit_bytes=12 * 1024 * 1024)
SMEM_SPEC = pl.BlockSpec(memory_space=pltpu.SMEM)


def iota(shape, dim):
    return lax.broadcasted_iota(i32, shape, dim)


def docs_along(starts_ref, shape, dim):
    positions = iota(shape, dim)
    total = jnp.zeros(shape, i32)
    for slot in range(starts_ref.shape[0]):
        total = total + (starts_ref[slot] <= positions).astype(i32)
    return total


def started_and_domain(starts_ref, domains_ref, row_count):
    slots = starts_ref.shape[0]
    started = jnp.int32(0)
    for slot in range(slots):
        started = started + (starts_ref[slot] < row_count).astype(i32)
    last_domain = jnp.int32(0)
    for slot in range(slots):
        last_domain = last_domain + jnp.where(slot == started - 1, domains_ref[slot], 0)
    return started, last_domain


def dot(a, b, contract):
    return lax.dot_general(a, b, (contract, ((), ())), preferred_element_type=f32)


def state_kernel(key_ref, value_ref, starts_ref, domains_ref, out_ref):
    row_count, width = key_ref.shape
    started, last_domain = started_and_domain(starts_ref, domains_ref, row_count)
    in_tail = docs_along(starts_ref, (row_count, HEAD_DIM), 0) == started
    for head in range(width // HEAD_DIM):
        cols = slice(head * HEAD_DIM, (head + 1) * HEAD_DIM)
        keys = jnp.where(in_tail, key_ref[:, cols].astype(f32), 0.0).astype(bf16)
        out_ref[:, 0, cols] = dot(keys, value_ref[:, cols], ((0,), (0,)))
    lane = iota((HEAD_DIM, LANES), 1)
    flag = (started > 0).astype(f32)
    out_ref[:, 0, width:] = jnp.where(
        lane == 0, flag, jnp.where(lane == 1, last_domain.astype(f32), 0.0)
    )


def carry_kernel(own_ref, states_ref, carried_ref, domain_ref, total_ref):
    total, blocks = states_ref.shape[0], carried_ref.shape[0]
    rows, heads = total // blocks, carried_ref.shape[1] // (total // blocks)
    width = heads * HEAD_DIM
    info = states_ref[0::rows, 0, width:] if rows > 1 else states_ref[:, 0, width:]
    flag_col = info[:, 0:1]
    domain_col = info[:, 1:2]
    here = iota((blocks, blocks), 0)
    there = iota((blocks, blocks), 1)
    flag_row = jnp.sum(jnp.where(here == there, flag_col, 0.0), axis=0, keepdims=True)
    latest = jnp.max(
        jnp.where((flag_row > 0.0) & (there < here), there, -1), axis=1, keepdims=True
    )
    joined = jnp.where((there < here) & (there >= latest), 1.0, 0.0).astype(bf16)
    for row in range(rows):
        for head in range(heads):
            cols = slice(head * HEAD_DIM, (head + 1) * HEAD_DIM)
            state = states_ref[row::rows, 0, cols] if rows > 1 else states_ref[:, 0, cols]
            high = state.astype(bf16)
            rest = state - high.astype(f32)
            middle = rest.astype(bf16)
            low = (rest - middle.astype(f32)).astype(bf16)
            summed = dot(joined, high, ((1,), (0,)))
            summed = summed + dot(joined, middle, ((1,), (0,)))
            summed = summed + dot(joined, low, ((1,), (0,)))
            total_ref[:, row * heads + head, :] = summed
    carried_ref[...] = total_ref[...].astype(bf16)
    block_ids = iota((blocks, 1), 0)
    before = (flag_col > 0.0) & (block_ids < own_ref[0])
    last_block = jnp.max(jnp.where(before, block_ids, -1))
    domain_ref[0] = jnp.sum(jnp.where(block_ids == last_block, domain_col, 0.0)).astype(i32)


def inner_kernel(query_ref, key_ref, value_ref, starts_ref, out_ref):
    row_count, width = query_ref.shape
    square = (row_count, row_count)
    visible = (iota(square, 1) <= iota(square, 0)) & (
        docs_along(starts_ref, square, 0) == docs_along(starts_ref, square, 1)
    )
    for head in range(width // HEAD_DIM):
        cols = slice(head * HEAD_DIM, (head + 1) * HEAD_DIM)
        scores = dot(query_ref[:, cols], key_ref[:, cols], ((1,), (1,)))
        scores = jnp.where(visible, scores, 0.0).astype(bf16)
        out_ref[:, cols] = dot(scores, value_ref[:, cols], ((1,), (0,)))


def attention_kernel(
    query_ref, inner_ref, carried_ref, gain_ref, starts_ref, domains_ref, weights_ref,
    domain_in_ref, out_ref, shared_ref, state_ref,
):
    row_count, width = query_ref.shape
    first_doc = docs_along(starts_ref, (row_count, HEAD_DIM), 0) == 0
    state_ref[...] = carried_ref[...].astype(f32)
    for head in range(width // HEAD_DIM):
        cols = slice(head * HEAD_DIM, (head + 1) * HEAD_DIM)
        state = state_ref[:, head, :].astype(bf16)
        part = dot(query_ref[:, cols], state, ((1,), (0,)))
        raw = inner_ref[:, cols] + jnp.where(first_doc, part, 0.0)
        scale = lax.rsqrt(jnp.mean(raw * raw, axis=1, keepdims=True) + 1e-05)
        normed = (raw * scale * gain_ref[:, cols]).astype(bf16)
        out_ref[:, cols] = normed
        shared_ref[:row_count, cols] = normed
    doc = docs_along(starts_ref, (16, row_count), 1)
    domain = jnp.where(doc == 0, domain_in_ref[0], 0)
    for slot in range(starts_ref.shape[0]):
        domain = jnp.where(doc == slot + 1, domains_ref[slot], domain)
    weight = jnp.zeros((16, row_count), f32)
    for which in range(weights_ref.shape[0]):
        weight = jnp.where(domain == which, weights_ref[which].astype(f32), weight)
    shared_ref[row_count:, :row_count] = weight.astype(bf16)
    shared_ref[row_count:, row_count:] = jnp.zeros((16, width - row_count), bf16)


def turn_kernel(cotangent_ref, core_ref, own_ref, other_ref, turned_ref, *, owned):
    width = cotangent_ref.shape[1]
    turned_ref[...] = cotangent_ref[...].T
    for core, out_ref in ((core_ref[0], own_ref), (1 - core_ref[0], other_ref)):
        for pair in range(width // (2 * owned)):
            start = pl.multiple_of(2 * pair * owned + core * owned, owned)
            out_ref[pair * owned : (pair + 1) * owned] = turned_ref[pl.ds(start, owned), :]


def gradient_kernel(place_ref, shared_ref, *refs):
    cotangent_refs, out_ref = refs[:-1], refs[-1]
    groups = len(cotangent_refs)
    _, cols, row_count = cotangent_refs[0].shape
    for shift, cotangent_ref in enumerate(cotangent_refs):
        total = None
        for side in range(2):
            core = jnp.where(side == 0, place_ref[0], 1 - place_ref[0])
            weight = shared_ref[core, row_count : row_count + 1, :row_count].astype(f32)
            weighted = (cotangent_ref[side].astype(f32) * weight).astype(bf16)
            part = dot(weighted, shared_ref[core, :row_count, :], ((1,), (0,)))
            total = part if total is None else total + part
        group = lax.rem(place_ref[1] - shift + groups, groups)
        out_ref[pl.ds(pl.multiple_of(group * cols, cols), cols), :] = total.astype(bf16)


def update_kernel(
    parts_ref, weight_ref, first_ref, second_ref, new_weight_ref, new_first_ref, new_second_ref
):
    gradient = jnp.sum(parts_ref[...].astype(f32), axis=0)
    weight = weight_ref[...]
    new_first = 0.9 * first_ref[...] + 0.1 * gradient
    new_second = 0.95 * second_ref[...] + 0.05 * gradient * gradient
    corrected_first = new_first / first_debias
    corrected_second = new_second / second_debias
    new_first_ref[...] = new_first
    new_second_ref[...] = new_second
    new_weight_ref[...] = weight - 0.01 * (
        corrected_first / (jnp.sqrt(corrected_second) + 1e-08) + 0.1 * weight
    )


def shape(dims, dtype):
    return jax.ShapeDtypeStruct(dims, dtype)


def on_device(
    queries, key_rows, value_rows, out_gain, doc_starts, doc_domains, domain_weights,
    cotangent, weight, moment_first, moment_second,
):
    chips, groups = lax.axis_size("chip"), lax.axis_size("group")
    blocks = 2 * chips
    row_count, width = queries.shape
    owned = weight.shape[1]
    rows, heads = HEAD_DIM // blocks, width // HEAD_DIM
    own_block = (lax.axis_index("chip") * 2 + lax.axis_index("core")).reshape(1).astype(i32)
    V, S = VMEM_SPEC, SMEM_SPEC

    place = jnp.stack([lax.axis_index("core"), lax.axis_index("group")]).astype(i32)
    own_half, other_half = pl.pallas_call(
        lambda *refs: turn_kernel(*refs, owned=owned),
        out_shape=(shape((width // 2, row_count), bf16),) * 2,
        in_specs=[V, S], out_specs=(V, V),
        scratch_shapes=[pltpu.VMEM((width, row_count), bf16)],
        compiler_params=SMALL, name="turn",
    )(cotangent, place)
    states = pl.pallas_call(
        state_kernel,
        out_shape=shape((HEAD_DIM, 1, width + LANES), f32),
        in_specs=[V, V, S, S], out_specs=V, compiler_params=SMALL, name="state",
    )(key_rows, value_rows, doc_starts, doc_domains)
    states = lax.all_to_all(states, ("chip", "core"), 0, 0, tiled=True)
    partner_half = lax.ppermute(other_half, "core", [(0, 1), (1, 0)])
    halves = jnp.stack([own_half, partner_half])
    turned = [halves] + [
        lax.ppermute(halves, "group", [(g, (g + k) % groups) for g in range(groups)])
        for k in range(1, groups)
    ]
    inner = pl.pallas_call(
        inner_kernel,
        out_shape=shape((row_count, width), f32),
        in_specs=[V, V, V, S], out_specs=V, compiler_params=SMALL, name="inner",
    )(queries, key_rows, value_rows, doc_starts)
    carried, domain_in = pl.pallas_call(
        carry_kernel,
        out_shape=(shape((blocks, rows * heads, HEAD_DIM), bf16), shape((1,), i32)),
        in_specs=[S, V], out_specs=(V, S),
        scratch_shapes=[pltpu.VMEM((blocks, rows * heads, HEAD_DIM), f32)],
        compiler_params=SMALL, name="carry",
    )(own_block, states)
    carried = lax.all_to_all(carried, ("chip", "core"), 0, 0, tiled=True)
    attention, shared = pl.pallas_call(
        attention_kernel,
        out_shape=(shape((row_count, width), bf16), shape((row_count + 16, width), bf16)),
        in_specs=[V, V, V, V, S, S, S, S], out_specs=(V, V),
        scratch_shapes=[pltpu.VMEM((HEAD_DIM, heads, HEAD_DIM), f32)],
        compiler_params=SMALL, name="attention",
    )(
        queries, inner, carried.reshape(HEAD_DIM, heads, HEAD_DIM), out_gain.reshape(1, width),
        doc_starts, doc_domains, domain_weights, domain_in,
    )
    shared = lax.all_gather(shared, "core", axis=0, tiled=False)
    partial = pl.pallas_call(
        gradient_kernel,
        out_shape=shape((groups * width // 2, width), bf16),
        in_specs=[S] + [V] * (1 + groups), out_specs=V,
        compiler_params=SMALL, name="gradient",
    )(place, shared, *turned)
    partial = partial.reshape(chips, owned, width)
    partial = lax.all_to_all(partial, "chip", 0, 0, tiled=True)
    new_weight, new_first, new_second = pl.pallas_call(
        update_kernel,
        out_shape=(shape((owned, width), f32),) * 3,
        in_specs=[V] * 4, out_specs=(V,) * 3, compiler_params=SMALL, name="update",
    )(partial, weight.T, moment_first.T, moment_second.T)
    return (attention, new_weight.T, new_first.T, new_second.T)


def solution(mesh):
    blocks, groups = mesh.devices.shape
    split = Mesh(mesh.devices.reshape(blocks // 2, 2, groups), ("chip", "core", "group"))
    seq, head = ("chip", "core"), "group"
    in_specs = (
        P(seq, head), P(seq, head), P(seq, head), P(head), P(seq), P(seq), P(),
        P(seq, head), P(head, seq), P(head, seq), P(head, seq),
    )
    out_specs = (P(seq, head), P(head, seq), P(head, seq), P(head, seq))
    return jax.shard_map(
        on_device, mesh=split, in_specs=in_specs, out_specs=out_specs, check_vma=False
    )
```

```python
import jax
import jax.numpy as jnp
from jax import lax
from jax.experimental import pallas as pl
from jax.experimental.pallas import tpu as pltpu
from jax.sharding import Mesh, PartitionSpec as P


HEAD_DIM = 128
LANES = 128

first_debias = 0.9999734386011124
second_debias = 0.994079470779666

f32, bf16, i32 = jnp.float32, jnp.bfloat16, jnp.int32
VMEM_SPEC = pl.BlockSpec(memory_space=pltpu.VMEM)
HBM_SPEC = pl.BlockSpec(memory_space=pltpu.HBM)
SMALL = pltpu.CompilerParams(vmem_limit_bytes=12 * 1024 * 1024)
SMEM_SPEC = pl.BlockSpec(memory_space=pltpu.SMEM)


def iota(shape, dim):
    return lax.broadcasted_iota(i32, shape, dim)


def docs_along(starts_ref, shape, dim):
    positions = iota(shape, dim)
    total = jnp.zeros(shape, i32)
    for slot in range(starts_ref.shape[0]):
        total = total + (starts_ref[slot] <= positions).astype(i32)
    return total


def started_and_domain(starts_ref, domains_ref, row_count):
    slots = starts_ref.shape[0]
    started = jnp.int32(0)
    for slot in range(slots):
        started = started + (starts_ref[slot] < row_count).astype(i32)
    last_domain = jnp.int32(0)
    for slot in range(slots):
        last_domain = last_domain + jnp.where(slot == started - 1, domains_ref[slot], 0)
    return started, last_domain


def dot(a, b, contract):
    return lax.dot_general(a, b, (contract, ((), ())), preferred_element_type=f32)


def state_kernel(
    key_hbm, value_hbm, starts_hbm, domains_hbm, out_ref,
    key_ref, value_ref, starts_ref, domains_ref, arrived,
):
    copies = [
        pltpu.make_async_copy(source, target, arrived.at[which])
        for which, (source, target) in enumerate((
            (starts_hbm, starts_ref), (domains_hbm, domains_ref),
            (key_hbm, key_ref), (value_hbm, value_ref),
        ))
    ]
    for copy in copies:
        copy.start()
    for copy in copies:
        copy.wait()
    row_count, width = key_ref.shape
    started, last_domain = started_and_domain(starts_ref, domains_ref, row_count)
    in_tail = docs_along(starts_ref, (row_count, HEAD_DIM), 0) == started
    for head in range(width // HEAD_DIM):
        cols = slice(head * HEAD_DIM, (head + 1) * HEAD_DIM)
        keys = jnp.where(in_tail, key_ref[:, cols].astype(f32), 0.0).astype(bf16)
        out_ref[:, 0, cols] = dot(keys, value_ref[:, cols], ((0,), (0,)))
    lane = iota((HEAD_DIM, LANES), 1)
    flag = (started > 0).astype(f32)
    out_ref[:, 0, width:] = jnp.where(
        lane == 0, flag, jnp.where(lane == 1, last_domain.astype(f32), 0.0)
    )


def carry_kernel(own_ref, weights_ref, states_ref, carried_ref, weight_ref, total_ref):
    total, blocks = states_ref.shape[0], carried_ref.shape[0]
    rows, heads = total // blocks, carried_ref.shape[1] // (total // blocks)
    width = heads * HEAD_DIM
    info = states_ref[0::rows, 0, width:] if rows > 1 else states_ref[:, 0, width:]
    flag_col = info[:, 0:1]
    domain_col = info[:, 1:2]
    here = iota((blocks, blocks), 0)
    there = iota((blocks, blocks), 1)
    flag_row = jnp.sum(jnp.where(here == there, flag_col, 0.0), axis=0, keepdims=True)
    latest = jnp.max(
        jnp.where((flag_row > 0.0) & (there < here), there, -1), axis=1, keepdims=True
    )
    joined = jnp.where((there < here) & (there >= latest), 1.0, 0.0).astype(bf16)
    for row in range(rows):
        state = states_ref[row::rows, 0, :width] if rows > 1 else states_ref[:, 0, :width]
        high = state.astype(bf16)
        rest = state - high.astype(f32)
        middle = rest.astype(bf16)
        low = (rest - middle.astype(f32)).astype(bf16)
        summed = dot(joined, high, ((1,), (0,)))
        summed = summed + dot(joined, middle, ((1,), (0,)))
        summed = summed + dot(joined, low, ((1,), (0,)))
        for head in range(heads):
            cols = slice(head * HEAD_DIM, (head + 1) * HEAD_DIM)
            total_ref[:, row * heads + head, :] = summed[:, cols]
    carried_ref[...] = total_ref[...].astype(bf16)
    block_ids = iota((blocks, 1), 0)
    before = (flag_col > 0.0) & (block_ids < own_ref[0])
    last_block = jnp.max(jnp.where(before, block_ids, -1))
    domain = jnp.sum(jnp.where(block_ids == last_block, domain_col, 0.0)).astype(i32)
    weight = jnp.int32(0)
    for which in range(weights_ref.shape[0]):
        weight = jnp.where(domain == which, weights_ref[which], weight)
    weight_ref[0] = weight


def inner_kernel(
    query_ref, key_ref, value_ref, gain_ref, starts_ref, domains_ref, weights_ref,
    out_ref, first_ref, lines_ref,
):
    row_count, width = query_ref.shape
    square = (row_count, row_count)
    down, along = docs_along(starts_ref, square, 0), docs_along(starts_ref, square, 1)
    visible = (iota(square, 1) <= iota(square, 0)) & (down == along)
    first_doc = down[:, :HEAD_DIM] == 0
    for head in range(width // HEAD_DIM):
        cols = slice(head * HEAD_DIM, (head + 1) * HEAD_DIM)
        query = query_ref[:, cols]
        scores = dot(query, key_ref[:, cols], ((1,), (1,)))
        scores = jnp.where(visible, scores, 0.0).astype(bf16)
        out_ref[:, cols] = dot(scores, value_ref[:, cols], ((1,), (0,)))
        first_ref[:, cols] = jnp.where(first_doc, query.astype(f32), 0.0).astype(bf16)
    doc = docs_along(starts_ref, (1, row_count), 1)
    line = jnp.zeros((1, row_count), i32)
    for slot in range(starts_ref.shape[0]):
        weight = jnp.int32(0)
        for which in range(weights_ref.shape[0]):
            weight = jnp.where(domains_ref[slot] == which, weights_ref[which], weight)
        line = jnp.where(doc == slot + 1, weight, line)
    lines_ref[...] = jnp.zeros(lines_ref.shape, f32)
    lines_ref[0:1, :] = gain_ref[...]
    lines_ref[1:2, :row_count] = line.astype(f32)


def attention_kernel(
    first_ref, inner_ref, carried_ref, lines_ref, weight_in_ref, out_ref, shared_ref, state_ref
):
    row_count, width = first_ref.shape
    state_ref[...] = carried_ref[...].astype(f32)
    for head in range(width // HEAD_DIM):
        cols = slice(head * HEAD_DIM, (head + 1) * HEAD_DIM)
        state = state_ref[:, head, :].astype(bf16)
        raw = inner_ref[:, cols] + dot(first_ref[:, cols], state, ((1,), (0,)))
        scale = lax.rsqrt(jnp.mean(raw * raw, axis=1, keepdims=True) + 1e-05)
        normed = (raw * scale * lines_ref[0:1, cols]).astype(bf16)
        out_ref[:, cols] = normed
        shared_ref[:row_count, cols] = normed
    line = lines_ref[1:2, :]
    line = jnp.where(line == 0.0, weight_in_ref[0].astype(f32), line)
    shared_ref[row_count:, :] = jnp.broadcast_to(line, (16, width)).astype(bf16)


def turn_kernel(cotangent_ref, core_ref, own_ref, other_ref, turned_ref, *, owned):
    width = cotangent_ref.shape[1]
    turned_ref[...] = cotangent_ref[...].T
    for core, out_ref in ((core_ref[0], own_ref), (1 - core_ref[0], other_ref)):
        for pair in range(width // (2 * owned)):
            start = pl.multiple_of(2 * pair * owned + core * owned, owned)
            out_ref[pair * owned : (pair + 1) * owned] = turned_ref[pl.ds(start, owned), :]


def gradient_kernel(place_ref, shared_ref, *refs):
    cotangent_refs, out_ref = refs[:-1], refs[-1]
    groups = len(cotangent_refs)
    _, cols, row_count = cotangent_refs[0].shape
    for shift, cotangent_ref in enumerate(cotangent_refs):
        total = None
        for side in range(2):
            core = jnp.where(side == 0, place_ref[0], 1 - place_ref[0])
            weight = shared_ref[core, row_count : row_count + 1, :row_count].astype(f32)
            weighted = (cotangent_ref[side].astype(f32) * weight).astype(bf16)
            part = dot(weighted, shared_ref[core, :row_count, :], ((1,), (0,)))
            total = part if total is None else total + part
        group = lax.rem(place_ref[1] - shift + groups, groups)
        out_ref[pl.ds(pl.multiple_of(group * cols, cols), cols), :] = total.astype(bf16)


def update_kernel(
    parts_ref, weight_ref, first_ref, second_ref, new_weight_ref, new_first_ref, new_second_ref
):
    gradient = jnp.sum(parts_ref[...].astype(f32), axis=0)
    weight = weight_ref[...]
    new_first = 0.9 * first_ref[...] + 0.1 * gradient
    new_second = 0.95 * second_ref[...] + 0.05 * gradient * gradient
    corrected_first = new_first / first_debias
    corrected_second = new_second / second_debias
    new_first_ref[...] = new_first
    new_second_ref[...] = new_second
    new_weight_ref[...] = weight - 0.01 * (
        corrected_first / (jnp.sqrt(corrected_second) + 1e-08) + 0.1 * weight
    )


def shape(dims, dtype):
    return jax.ShapeDtypeStruct(dims, dtype)


def on_device(
    queries, key_rows, value_rows, out_gain, doc_starts, doc_domains, domain_weights,
    cotangent, weight, moment_first, moment_second,
):
    chips, groups = lax.axis_size("chip"), lax.axis_size("group")
    blocks = 2 * chips
    row_count, width = queries.shape
    owned = weight.shape[1]
    rows, heads = HEAD_DIM // blocks, width // HEAD_DIM
    own_block = (lax.axis_index("chip") * 2 + lax.axis_index("core")).reshape(1).astype(i32)
    V, S = VMEM_SPEC, SMEM_SPEC

    place = jnp.stack([lax.axis_index("core"), lax.axis_index("group")]).astype(i32)
    own_half, other_half = pl.pallas_call(
        lambda *refs: turn_kernel(*refs, owned=owned),
        out_shape=(shape((width // 2, row_count), bf16),) * 2,
        in_specs=[V, S], out_specs=(V, V),
        scratch_shapes=[pltpu.VMEM((width, row_count), bf16)],
        compiler_params=SMALL, name="turn",
    )(cotangent, place)
    states = pl.pallas_call(
        state_kernel,
        out_shape=shape((HEAD_DIM, 1, width + LANES), f32),
        in_specs=[HBM_SPEC] * 4, out_specs=V,
        scratch_shapes=[
            pltpu.VMEM(key_rows.shape, bf16), pltpu.VMEM(value_rows.shape, bf16),
            pltpu.SMEM(doc_starts.shape, i32), pltpu.SMEM(doc_domains.shape, i32),
            pltpu.SemaphoreType.DMA((4,)),
        ],
        compiler_params=SMALL, name="state",
    )(*(
        pltpu.with_memory_space_constraint(operand, pltpu.HBM)
        for operand in (key_rows, value_rows, doc_starts, doc_domains)
    ))
    states = lax.all_to_all(states, ("chip", "core"), 0, 0, tiled=True)
    partner_half = lax.ppermute(other_half, "core", [(0, 1), (1, 0)])
    halves = jnp.stack([own_half, partner_half])
    turned = [halves]
    for k in range(1, groups):
        turned.append(lax.ppermute(halves, "group", [(g, (g + k) % groups) for g in range(groups)]))
    inner, first, lines = pl.pallas_call(
        inner_kernel,
        out_shape=(
            shape((row_count, width), f32), shape((row_count, width), bf16), shape((8, width), f32)
        ),
        in_specs=[V, V, V, V, S, S, S], out_specs=(V, V, V),
        compiler_params=SMALL, name="inner",
    )(
        queries, key_rows, value_rows, out_gain.reshape(1, width),
        doc_starts, doc_domains, domain_weights,
    )
    carry_call = pl.pallas_call(
        carry_kernel,
        out_shape=(shape((blocks, rows * heads, HEAD_DIM), bf16), shape((1,), i32)),
        in_specs=[S, S, V], out_specs=(V, S),
        scratch_shapes=[pltpu.VMEM((blocks, rows * heads, HEAD_DIM), f32)],
        compiler_params=SMALL, name="carry",
    )
    carried, weight_in = carry_call(own_block, domain_weights, states)
    carried = lax.all_to_all(carried, ("chip", "core"), 0, 0, tiled=True)
    attention, shared = pl.pallas_call(
        attention_kernel,
        out_shape=(shape((row_count, width), bf16), shape((row_count + 16, width), bf16)),
        in_specs=[V, V, V, V, S], out_specs=(V, V),
        scratch_shapes=[pltpu.VMEM((HEAD_DIM, heads, HEAD_DIM), f32)],
        compiler_params=SMALL, name="attention",
    )(first, inner, carried.reshape(HEAD_DIM, heads, HEAD_DIM), lines, weight_in)
    shared = lax.all_gather(shared, "core", axis=0, tiled=False)
    partial = pl.pallas_call(
        gradient_kernel,
        out_shape=shape((groups * width // 2, width), bf16),
        in_specs=[S] + [V] * (1 + groups), out_specs=V,
        compiler_params=SMALL, name="gradient",
    )(place, shared, *turned)
    partial = partial.reshape(chips, owned, width)
    partial = lax.all_to_all(partial, "chip", 0, 0, tiled=True)
    new_weight, new_first, new_second = pl.pallas_call(
        update_kernel,
        out_shape=(shape((owned, width), f32),) * 3,
        in_specs=[V] * 4, out_specs=(V,) * 3, compiler_params=SMALL, name="update",
    )(partial, weight.T, moment_first.T, moment_second.T)
    return (attention, new_weight.T, new_first.T, new_second.T)


def solution(mesh):
    blocks, groups = mesh.devices.shape
    split = Mesh(mesh.devices.reshape(blocks // 2, 2, groups), ("chip", "core", "group"))
    seq, head = ("chip", "core"), "group"
    in_specs = (
        P(seq, head), P(seq, head), P(seq, head), P(head), P(seq), P(seq), P(),
        P(seq, head), P(head, seq), P(head, seq), P(head, seq),
    )
    out_specs = (P(seq, head), P(head, seq), P(head, seq), P(head, seq))
    return jax.shard_map(
        on_device, mesh=split, in_specs=in_specs, out_specs=out_specs, check_vma=False
    )
```

```python
import math

import jax
import jax.numpy as jnp
from jax import lax
from jax.experimental import pallas as pl
from jax.experimental.pallas import tpu as pltpu
from jax.sharding import Mesh, PartitionSpec as P


HEAD_DIM = 128
LANES = 128

first_debias = 0.9999734386011124
second_debias = 0.994079470779666

f32, bf16, i32 = jnp.float32, jnp.bfloat16, jnp.int32
VMEM_SPEC = pl.BlockSpec(memory_space=pltpu.VMEM)
HBM_SPEC = pl.BlockSpec(memory_space=pltpu.HBM)
SMALL = pltpu.CompilerParams(vmem_limit_bytes=12 * 1024 * 1024)
SMEM_SPEC = pl.BlockSpec(memory_space=pltpu.SMEM)


def iota(shape, dim):
    return lax.broadcasted_iota(i32, shape, dim)


def docs_along(starts_ref, shape, dim):
    positions = iota(shape, dim)
    total = jnp.zeros(shape, i32)
    for slot in range(starts_ref.shape[0]):
        total = total + (starts_ref[slot] <= positions).astype(i32)
    return total


def started_and_domain(starts_ref, domains_ref, row_count):
    slots = starts_ref.shape[0]
    started = jnp.int32(0)
    for slot in range(slots):
        started = started + (starts_ref[slot] < row_count).astype(i32)
    last_domain = jnp.int32(0)
    for slot in range(slots):
        last_domain = last_domain + jnp.where(slot == started - 1, domains_ref[slot], 0)
    return started, last_domain


def dot(a, b, contract):
    return lax.dot_general(a, b, (contract, ((), ())), preferred_element_type=f32)


def state_kernel(
    key_hbm, value_hbm, starts_hbm, domains_hbm, out_ref,
    key_ref, value_ref, starts_ref, domains_ref, arrived,
):
    copies = [
        pltpu.make_async_copy(source, target, arrived.at[which])
        for which, (source, target) in enumerate((
            (starts_hbm, starts_ref), (domains_hbm, domains_ref),
            (key_hbm, key_ref), (value_hbm, value_ref),
        ))
    ]
    for copy in copies:
        copy.start()
    for copy in copies:
        copy.wait()
    row_count, width = key_ref.shape
    started, last_domain = started_and_domain(starts_ref, domains_ref, row_count)
    in_tail = docs_along(starts_ref, (row_count, HEAD_DIM), 0) == started
    for head in range(width // HEAD_DIM):
        cols = slice(head * HEAD_DIM, (head + 1) * HEAD_DIM)
        keys = jnp.where(in_tail, key_ref[:, cols].astype(f32), 0.0).astype(bf16)
        out_ref[:, 0, cols] = dot(keys, value_ref[:, cols], ((0,), (0,)))
    lane = iota((HEAD_DIM, LANES), 1)
    flag = (started > 0).astype(f32)
    out_ref[:, 0, width:] = jnp.where(
        lane == 0, flag, jnp.where(lane == 1, last_domain.astype(f32), 0.0)
    )


def carry_kernel(weights_ref, states_ref, carried_ref, weight_ref, total_ref):
    total, blocks = states_ref.shape[0], carried_ref.shape[0]
    rows, heads = total // blocks, carried_ref.shape[1] // (total // blocks)
    width = heads * HEAD_DIM
    info = states_ref[0::rows, 0, width:] if rows > 1 else states_ref[:, 0, width:]
    flag_col = info[:, 0:1]
    domain_col = info[:, 1:2]
    here = iota((blocks, blocks), 0)
    there = iota((blocks, blocks), 1)
    flag_row = jnp.sum(jnp.where(here == there, flag_col, 0.0), axis=0, keepdims=True)
    latest = jnp.max(
        jnp.where((flag_row > 0.0) & (there < here), there, -1), axis=1, keepdims=True
    )
    joined = jnp.where((there < here) & (there >= latest), 1.0, 0.0).astype(bf16)
    for row in range(rows):
        for head in range(heads):
            cols = slice(head * HEAD_DIM, (head + 1) * HEAD_DIM)
            state = states_ref[row::rows, 0, cols] if rows > 1 else states_ref[:, 0, cols]
            high = state.astype(bf16)
            rest = state - high.astype(f32)
            middle = rest.astype(bf16)
            low = (rest - middle.astype(f32)).astype(bf16)
            summed = dot(joined, high, ((1,), (0,)))
            summed = summed + dot(joined, middle, ((1,), (0,)))
            summed = summed + dot(joined, low, ((1,), (0,)))
            total_ref[:, row * heads + head, :] = summed
    carried_ref[...] = total_ref[...].astype(bf16)
    own = lax.axis_index("chip") * 2 + lax.axis_index("core")
    block_ids = iota((blocks, 1), 0)
    before = (flag_col > 0.0) & (block_ids < own)
    last_block = jnp.max(jnp.where(before, block_ids, -1), axis=0, keepdims=True)
    domain = jnp.sum(jnp.where(block_ids == last_block, domain_col, 0.0), axis=0, keepdims=True)
    slot = iota(weights_ref.shape, 1).astype(f32)
    weight = jnp.sum(
        jnp.where(slot == domain, weights_ref[...].astype(f32), 0.0), axis=1, keepdims=True
    )
    weight_ref[...] = jnp.broadcast_to(weight, weight_ref.shape)


def inner_kernel(
    query_ref, key_ref, value_ref, gain_ref, starts_ref, domains_ref, weights_ref,
    out_ref, first_ref, lines_ref,
):
    row_count, width = query_ref.shape
    square = (row_count, row_count)
    down, along = docs_along(starts_ref, square, 0), docs_along(starts_ref, square, 1)
    visible = (iota(square, 1) <= iota(square, 0)) & (down == along)
    first_doc = down[:, :HEAD_DIM] == 0
    for head in range(width // HEAD_DIM):
        cols = slice(head * HEAD_DIM, (head + 1) * HEAD_DIM)
        query = query_ref[:, cols]
        scores = dot(query, key_ref[:, cols], ((1,), (1,)))
        scores = jnp.where(visible, scores, 0.0).astype(bf16)
        out_ref[:, cols] = dot(scores, value_ref[:, cols], ((1,), (0,)))
        first_ref[:, cols] = jnp.where(first_doc, query.astype(f32), 0.0).astype(bf16)
    doc = docs_along(starts_ref, (1, row_count), 1)
    line = jnp.zeros((1, row_count), i32)
    for slot in range(starts_ref.shape[0]):
        weight = jnp.int32(0)
        for which in range(weights_ref.shape[0]):
            weight = jnp.where(domains_ref[slot] == which, weights_ref[which], weight)
        line = jnp.where(doc == slot + 1, weight, line)
    lines_ref[...] = jnp.zeros(lines_ref.shape, f32)
    lines_ref[0:1, :] = gain_ref[...]
    lines_ref[1:2, :row_count] = line.astype(f32)


def attention_kernel(
    first_ref, inner_ref, carried_ref, lines_ref, weight_in_ref, shared_ref, state_ref
):
    row_count, width = first_ref.shape
    state_ref[...] = carried_ref[...].astype(f32)
    for head in range(width // HEAD_DIM):
        cols = slice(head * HEAD_DIM, (head + 1) * HEAD_DIM)
        state = state_ref[:, head, :].astype(bf16)
        raw = inner_ref[:, cols] + dot(first_ref[:, cols], state, ((1,), (0,)))
        scale = lax.rsqrt(jnp.mean(raw * raw, axis=1, keepdims=True) + 1e-05)
        shared_ref[:row_count, cols] = (raw * scale * lines_ref[0:1, cols]).astype(bf16)
    line = lines_ref[1:2, :]
    line = jnp.where(line == 0.0, weight_in_ref[0:1, 0:1], line)
    shared_ref[row_count:, :] = jnp.broadcast_to(line, (16, width)).astype(bf16)


def turn_kernel(cotangent_ref, core_ref, own_ref, other_ref, turned_ref, *, owned):
    width = cotangent_ref.shape[1]
    turned_ref[...] = cotangent_ref[...].T
    for core, out_ref in ((core_ref[0], own_ref), (1 - core_ref[0], other_ref)):
        for pair in range(width // (2 * owned)):
            start = pl.multiple_of(2 * pair * owned + core * owned, owned)
            out_ref[pair * owned : (pair + 1) * owned] = turned_ref[pl.ds(start, owned), :]


def gradient_kernel(shared_ref, *refs, owned, side):
    cotangent_refs, (out_ref, attention_ref, sent) = refs[:-3], refs[-3:]
    groups = len(cotangent_refs)
    _, cols, row_count = cotangent_refs[0].shape
    core, own_group = lax.axis_index("core"), lax.axis_index("group")
    save = pltpu.make_async_copy(shared_ref.at[core, :row_count], attention_ref, sent)
    save.start()
    for shift, cotangent_ref in enumerate(cotangent_refs):
        total = None
        for which in (core, 1 - core):
            near = 0 if total is None else 1
            weight = shared_ref[which, row_count : row_count + 1, :row_count].astype(f32)
            weighted = (cotangent_ref[near].astype(f32) * weight).astype(bf16)
            part = dot(weighted, shared_ref[which, :row_count, :], ((1,), (0,)))
            total = part if total is None else total + part
        total = total.astype(bf16)
        group = lax.rem(own_group - shift + groups, groups)
        for block in range(cols // owned):
            owner = group * (cols // owned) + block
            down, along = owner // side, lax.rem(owner, side)
            place = jnp.where(core == 0, along * side + down, owner)
            out_ref[pl.ds(pl.multiple_of(place * owned, owned), owned), :] = total[
                block * owned : (block + 1) * owned
            ]
    save.wait()


def sum_kernel(parts_ref, out_ref):
    out_ref[...] = jnp.sum(parts_ref[...].astype(f32), axis=0).astype(bf16)


def update_kernel(
    parts_ref, weight_ref, first_ref, second_ref, new_weight_ref, new_first_ref, new_second_ref
):
    gradient = jnp.sum(parts_ref[...].astype(f32), axis=0)
    weight = weight_ref[...]
    new_first = 0.9 * first_ref[...] + 0.1 * gradient
    new_second = 0.95 * second_ref[...] + 0.05 * gradient * gradient
    corrected_first = new_first / first_debias
    corrected_second = new_second / second_debias
    new_first_ref[...] = new_first
    new_second_ref[...] = new_second
    new_weight_ref[...] = weight - 0.01 * (
        corrected_first / (jnp.sqrt(corrected_second) + 1e-08) + 0.1 * weight
    )


def shape(dims, dtype):
    return jax.ShapeDtypeStruct(dims, dtype)


def on_device(
    queries, key_rows, value_rows, out_gain, doc_starts, doc_domains, domain_weights,
    cotangent, weight, moment_first, moment_second,
):
    chips, groups = lax.axis_size("chip"), lax.axis_size("group")
    blocks = 2 * chips
    row_count, width = queries.shape
    owned = weight.shape[1]
    rows, heads = HEAD_DIM // blocks, width // HEAD_DIM
    V, S = VMEM_SPEC, SMEM_SPEC

    core, group = lax.axis_index("core"), lax.axis_index("group")
    place = jnp.stack([core, group]).astype(i32)
    own_half, other_half = pl.pallas_call(
        lambda *refs: turn_kernel(*refs, owned=owned),
        out_shape=(shape((width // 2, row_count), bf16),) * 2,
        in_specs=[V, S], out_specs=(V, V),
        scratch_shapes=[pltpu.VMEM((width, row_count), bf16)],
        compiler_params=SMALL, name="turn",
    )(cotangent, place)
    states = pl.pallas_call(
        state_kernel,
        out_shape=pltpu.VMEM((HEAD_DIM, 1, width + LANES), f32),
        in_specs=[HBM_SPEC] * 4, out_specs=V,
        scratch_shapes=[
            pltpu.VMEM(key_rows.shape, bf16), pltpu.VMEM(value_rows.shape, bf16),
            pltpu.SMEM(doc_starts.shape, i32), pltpu.SMEM(doc_domains.shape, i32),
            pltpu.SemaphoreType.DMA((4,)),
        ],
        compiler_params=SMALL, name="state",
    )(*(
        pltpu.with_memory_space_constraint(operand, pltpu.HBM)
        for operand in (key_rows, value_rows, doc_starts, doc_domains)
    ))
    states = lax.all_to_all(states, ("chip", "core"), 0, 0, tiled=True)
    partner_half = lax.ppermute(other_half, "core", [(0, 1), (1, 0)])
    halves = jnp.stack([own_half, partner_half])
    turned = [halves]
    for k in range(1, groups):
        turned.append(lax.ppermute(halves, "group", [(g, (g + k) % groups) for g in range(groups)]))
    inner, first, lines = pl.pallas_call(
        inner_kernel,
        out_shape=(
            shape((row_count, width), f32), shape((row_count, width), bf16), shape((8, width), f32)
        ),
        in_specs=[V, V, V, V, S, S, S], out_specs=(V, V, V),
        compiler_params=SMALL, name="inner",
    )(
        queries, key_rows, value_rows, out_gain.reshape(1, width),
        doc_starts, doc_domains, domain_weights,
    )
    carry_call = pl.pallas_call(
        carry_kernel,
        out_shape=(
            pltpu.VMEM((blocks, rows * heads, HEAD_DIM), bf16), shape((8, LANES), f32),
        ),
        in_specs=[V, V], out_specs=(V, V),
        scratch_shapes=[pltpu.VMEM((blocks, rows * heads, HEAD_DIM), f32)],
        compiler_params=SMALL, name="carry",
    )
    carried, weight_in = carry_call(domain_weights.reshape(1, -1), states)
    carried = lax.all_to_all(carried, ("chip", "core"), 0, 0, tiled=True)
    shared = pl.pallas_call(
        attention_kernel,
        out_shape=shape((row_count + 16, width), bf16),
        in_specs=[V] * 5, out_specs=V,
        scratch_shapes=[pltpu.VMEM((HEAD_DIM, heads, HEAD_DIM), f32)],
        compiler_params=SMALL, name="attention",
    )(first, inner, carried.reshape(HEAD_DIM, heads, HEAD_DIM), lines, weight_in)
    shared = lax.all_gather(shared, "core", axis=0, tiled=False)
    side = math.isqrt(chips)
    partial, attention = pl.pallas_call(
        lambda *refs: gradient_kernel(*refs, owned=owned, side=side),
        out_shape=(
            shape((groups * width // 2, width), bf16), shape((row_count, width), bf16)
        ),
        in_specs=[V] * (1 + groups), out_specs=(V, HBM_SPEC),
        scratch_shapes=[pltpu.SemaphoreType.DMA],
        compiler_params=SMALL, name="gradient",
    )(shared, *turned)
    lines_of = [
        [[(y * side + z) * 2 + c for z in range(side)] for y in range(side)] for c in range(2)
    ]
    rows_of = [[list(line) for line in zip(*lines)] for lines in lines_of]
    partial = lax.all_to_all(
        partial.reshape(side, side * owned, width), ("chip", "core"), 0, 0, tiled=True,
        axis_index_groups=lines_of[0] + rows_of[1],
    )
    partial = pl.pallas_call(
        sum_kernel,
        out_shape=shape((side * owned, width), bf16),
        in_specs=[V], out_specs=V, compiler_params=SMALL, name="sum",
    )(partial)
    partial = lax.all_to_all(
        partial.reshape(side, owned, width), ("chip", "core"), 0, 0, tiled=True,
        axis_index_groups=rows_of[0] + lines_of[1],
    )
    new_weight, new_first, new_second = pl.pallas_call(
        update_kernel,
        out_shape=(shape((owned, width), f32),) * 3,
        in_specs=[V] * 4, out_specs=(V,) * 3, compiler_params=SMALL, name="update",
    )(partial, weight.T, moment_first.T, moment_second.T)
    return (attention, new_weight.T, new_first.T, new_second.T)


def solution(mesh):
    blocks, groups = mesh.devices.shape
    split = Mesh(mesh.devices.reshape(blocks // 2, 2, groups), ("chip", "core", "group"))
    seq, head = ("chip", "core"), "group"
    in_specs = (
        P(seq, head), P(seq, head), P(seq, head), P(head), P(seq), P(seq), P(),
        P(seq, head), P(head, seq), P(head, seq), P(head, seq),
    )
    out_specs = (P(seq, head), P(head, seq), P(head, seq), P(head, seq))
    return jax.shard_map(
        on_device, mesh=split, in_specs=in_specs, out_specs=out_specs, check_vma=False
    )
```

```python
import math

import jax
import jax.numpy as jnp
from jax import lax
from jax.experimental import pallas as pl
from jax.experimental.pallas import tpu as pltpu
from jax.sharding import Mesh, PartitionSpec as P


HEAD_DIM = 128
LANES = 128

first_debias = 0.9999734386011124
second_debias = 0.994079470779666

f32, bf16, i32 = jnp.float32, jnp.bfloat16, jnp.int32
VMEM_SPEC = pl.BlockSpec(memory_space=pltpu.VMEM)
HBM_SPEC = pl.BlockSpec(memory_space=pltpu.HBM)
SMALL = pltpu.CompilerParams(vmem_limit_bytes=12 * 1024 * 1024)
SMEM_SPEC = pl.BlockSpec(memory_space=pltpu.SMEM)


def iota(shape, dim):
    return lax.broadcasted_iota(i32, shape, dim)


def docs_along(starts_ref, shape, dim):
    positions = iota(shape, dim)
    total = jnp.zeros(shape, i32)
    for slot in range(starts_ref.shape[0]):
        total = total + (starts_ref[slot] <= positions).astype(i32)
    return total


def started_and_domain(starts_ref, domains_ref, row_count):
    slots = starts_ref.shape[0]
    started = jnp.int32(0)
    for slot in range(slots):
        started = started + (starts_ref[slot] < row_count).astype(i32)
    last_domain = jnp.int32(0)
    for slot in range(slots):
        last_domain = last_domain + jnp.where(slot == started - 1, domains_ref[slot], 0)
    return started, last_domain


def dot(a, b, contract):
    return lax.dot_general(a, b, (contract, ((), ())), preferred_element_type=f32)


def state_kernel(
    key_hbm, value_hbm, starts_hbm, domains_hbm, out_ref,
    key_ref, value_ref, starts_ref, domains_ref, arrived,
):
    copies = [
        pltpu.make_async_copy(source, target, arrived.at[which])
        for which, (source, target) in enumerate((
            (starts_hbm, starts_ref), (domains_hbm, domains_ref),
            (key_hbm, key_ref), (value_hbm, value_ref),
        ))
    ]
    for copy in copies:
        copy.start()
    for copy in copies:
        copy.wait()
    row_count, width = key_ref.shape
    started, last_domain = started_and_domain(starts_ref, domains_ref, row_count)
    in_tail = docs_along(starts_ref, (row_count, HEAD_DIM), 0) == started
    for head in range(width // HEAD_DIM):
        cols = slice(head * HEAD_DIM, (head + 1) * HEAD_DIM)
        keys = jnp.where(in_tail, key_ref[:, cols].astype(f32), 0.0).astype(bf16)
        out_ref[:, 0, cols] = dot(keys, value_ref[:, cols], ((0,), (0,)))
    lane = iota((HEAD_DIM, LANES), 1)
    flag = (started > 0).astype(f32)
    out_ref[:, 0, width:] = jnp.where(
        lane == 0, flag, jnp.where(lane == 1, last_domain.astype(f32), 0.0)
    )


def carry_kernel(weights_ref, states_ref, carried_ref, weight_ref, total_ref):
    total, blocks = states_ref.shape[0], carried_ref.shape[0]
    rows, heads = total // blocks, carried_ref.shape[1] // (total // blocks)
    width = heads * HEAD_DIM
    info = states_ref[0::rows, 0, width:] if rows > 1 else states_ref[:, 0, width:]
    flag_col = info[:, 0:1]
    domain_col = info[:, 1:2]
    here = iota((blocks, blocks), 0)
    there = iota((blocks, blocks), 1)
    flag_row = jnp.sum(jnp.where(here == there, flag_col, 0.0), axis=0, keepdims=True)
    latest = jnp.max(
        jnp.where((flag_row > 0.0) & (there < here), there, -1), axis=1, keepdims=True
    )
    joined = jnp.where((there < here) & (there >= latest), 1.0, 0.0).astype(bf16)
    for row in range(rows):
        for head in range(heads):
            cols = slice(head * HEAD_DIM, (head + 1) * HEAD_DIM)
            state = states_ref[row::rows, 0, cols] if rows > 1 else states_ref[:, 0, cols]
            high = state.astype(bf16)
            rest = state - high.astype(f32)
            middle = rest.astype(bf16)
            low = (rest - middle.astype(f32)).astype(bf16)
            summed = dot(joined, high, ((1,), (0,)))
            summed = summed + dot(joined, middle, ((1,), (0,)))
            summed = summed + dot(joined, low, ((1,), (0,)))
            total_ref[:, row * heads + head, :] = summed
    carried_ref[...] = total_ref[...].astype(bf16)
    own = lax.axis_index("chip") * 2 + lax.axis_index("core")
    block_ids = iota((blocks, 1), 0)
    before = (flag_col > 0.0) & (block_ids < own)
    last_block = jnp.max(jnp.where(before, block_ids, -1), axis=0, keepdims=True)
    domain = jnp.sum(jnp.where(block_ids == last_block, domain_col, 0.0), axis=0, keepdims=True)
    slot = iota(weights_ref.shape, 1).astype(f32)
    weight = jnp.sum(
        jnp.where(slot == domain, weights_ref[...].astype(f32), 0.0), axis=1, keepdims=True
    )
    weight_ref[...] = jnp.broadcast_to(weight, weight_ref.shape)


def inner_kernel(
    query_ref, key_ref, value_ref, gain_ref, starts_ref, domains_ref, weights_ref,
    out_ref, first_ref, lines_ref,
):
    row_count, width = query_ref.shape
    square = (row_count, row_count)
    down, along = docs_along(starts_ref, square, 0), docs_along(starts_ref, square, 1)
    visible = (iota(square, 1) <= iota(square, 0)) & (down == along)
    first_doc = down[:, :HEAD_DIM] == 0
    for head in range(width // HEAD_DIM):
        cols = slice(head * HEAD_DIM, (head + 1) * HEAD_DIM)
        query = query_ref[:, cols]
        scores = dot(query, key_ref[:, cols], ((1,), (1,)))
        scores = jnp.where(visible, scores, 0.0).astype(bf16)
        out_ref[:, cols] = dot(scores, value_ref[:, cols], ((1,), (0,)))
        first_ref[:, cols] = jnp.where(first_doc, query.astype(f32), 0.0).astype(bf16)
    doc = docs_along(starts_ref, (1, row_count), 1)
    line = jnp.zeros((1, row_count), i32)
    for slot in range(starts_ref.shape[0]):
        weight = jnp.int32(0)
        for which in range(weights_ref.shape[0]):
            weight = jnp.where(domains_ref[slot] == which, weights_ref[which], weight)
        line = jnp.where(doc == slot + 1, weight, line)
    lines_ref[...] = jnp.zeros(lines_ref.shape, f32)
    lines_ref[0:1, :] = gain_ref[...]
    lines_ref[1:2, :row_count] = line.astype(f32)


def attention_kernel(
    first_ref, inner_ref, carried_ref, lines_ref, weight_in_ref, shared_ref, state_ref
):
    row_count, width = first_ref.shape
    state_ref[...] = carried_ref[...].astype(f32)
    for head in range(width // HEAD_DIM):
        cols = slice(head * HEAD_DIM, (head + 1) * HEAD_DIM)
        state = state_ref[:, head, :].astype(bf16)
        raw = inner_ref[:, cols] + dot(first_ref[:, cols], state, ((1,), (0,)))
        scale = lax.rsqrt(jnp.mean(raw * raw, axis=1, keepdims=True) + 1e-05)
        shared_ref[:row_count, cols] = (raw * scale * lines_ref[0:1, cols]).astype(bf16)
    line = lines_ref[1:2, :]
    line = jnp.where(line == 0.0, weight_in_ref[0:1, 0:1], line)
    shared_ref[row_count:, :] = jnp.broadcast_to(line, (16, width)).astype(bf16)


def turn_kernel(cotangent_ref, own_ref, other_ref, turned_ref, *, owned):
    width = cotangent_ref.shape[1]
    turned_ref[...] = cotangent_ref[...].T
    own = lax.axis_index("core")
    for core, out_ref in ((own, own_ref), (1 - own, other_ref)):
        for pair in range(width // (2 * owned)):
            start = pl.multiple_of(2 * pair * owned + core * owned, owned)
            out_ref[pair * owned : (pair + 1) * owned] = turned_ref[pl.ds(start, owned), :]


def gradient_kernel(shared_ref, *refs, owned, side):
    cotangent_refs, (out_ref, attention_ref, sent) = refs[:-3], refs[-3:]
    groups = len(cotangent_refs)
    _, cols, row_count = cotangent_refs[0].shape
    core, own_group = lax.axis_index("core"), lax.axis_index("group")
    save = pltpu.make_async_copy(shared_ref.at[core, :row_count], attention_ref, sent)
    save.start()
    for shift, cotangent_ref in enumerate(cotangent_refs):
        total = None
        for which in (core, 1 - core):
            near = 0 if total is None else 1
            weight = shared_ref[which, row_count : row_count + 1, :row_count].astype(f32)
            weighted = (cotangent_ref[near].astype(f32) * weight).astype(bf16)
            part = dot(weighted, shared_ref[which, :row_count, :], ((1,), (0,)))
            total = part if total is None else total + part
        total = total.astype(bf16)
        group = lax.rem(own_group - shift + groups, groups)
        for block in range(cols // owned):
            owner = group * (cols // owned) + block
            down, along = owner // side, lax.rem(owner, side)
            place = jnp.where(core == 0, along * side + down, owner)
            out_ref[pl.ds(pl.multiple_of(place * owned, owned), owned), :] = total[
                block * owned : (block + 1) * owned
            ]
    save.wait()


def sum_kernel(parts_ref, out_ref):
    out_ref[...] = jnp.sum(parts_ref[...].astype(f32), axis=0).astype(bf16)


def update_kernel(
    parts_ref, weight_ref, first_ref, second_ref, new_weight_ref, new_first_ref, new_second_ref
):
    gradient = jnp.sum(parts_ref[...].astype(f32), axis=0)
    weight = weight_ref[...]
    new_first = 0.9 * first_ref[...] + 0.1 * gradient
    new_second = 0.95 * second_ref[...] + 0.05 * gradient * gradient
    corrected_first = new_first / first_debias
    corrected_second = new_second / second_debias
    new_first_ref[...] = new_first
    new_second_ref[...] = new_second
    new_weight_ref[...] = weight - 0.01 * (
        corrected_first / (jnp.sqrt(corrected_second) + 1e-08) + 0.1 * weight
    )


def shape(dims, dtype):
    return jax.ShapeDtypeStruct(dims, dtype)


def on_device(
    queries, key_rows, value_rows, out_gain, doc_starts, doc_domains, domain_weights,
    cotangent, weight, moment_first, moment_second,
):
    chips, groups = lax.axis_size("chip"), lax.axis_size("group")
    blocks = 2 * chips
    row_count, width = queries.shape
    owned = weight.shape[1]
    rows, heads = HEAD_DIM // blocks, width // HEAD_DIM
    V, S = VMEM_SPEC, SMEM_SPEC

    own_half, other_half = pl.pallas_call(
        lambda *refs: turn_kernel(*refs, owned=owned),
        out_shape=(shape((width // 2, row_count), bf16),) * 2,
        in_specs=[V], out_specs=(V, V),
        scratch_shapes=[pltpu.VMEM((width, row_count), bf16)],
        compiler_params=SMALL, name="turn",
    )(cotangent)
    states = pl.pallas_call(
        state_kernel,
        out_shape=pltpu.VMEM((HEAD_DIM, 1, width + LANES), f32),
        in_specs=[HBM_SPEC] * 4, out_specs=V,
        scratch_shapes=[
            pltpu.VMEM(key_rows.shape, bf16), pltpu.VMEM(value_rows.shape, bf16),
            pltpu.SMEM(doc_starts.shape, i32), pltpu.SMEM(doc_domains.shape, i32),
            pltpu.SemaphoreType.DMA((4,)),
        ],
        compiler_params=SMALL, name="state",
    )(*(
        pltpu.with_memory_space_constraint(operand, pltpu.HBM)
        for operand in (key_rows, value_rows, doc_starts, doc_domains)
    ))
    states = lax.all_to_all(states, ("chip", "core"), 0, 0, tiled=True)
    partner_half = lax.ppermute(other_half, "core", [(0, 1), (1, 0)])
    halves = jnp.stack([own_half, partner_half])
    turned = [halves]
    for k in range(1, groups):
        turned.append(lax.ppermute(halves, "group", [(g, (g + k) % groups) for g in range(groups)]))
    inner_call = pl.pallas_call(
        inner_kernel,
        out_shape=(
            shape((row_count, width), f32), shape((row_count, width), bf16), shape((8, width), f32)
        ),
        in_specs=[V, V, V, V, S, S, S], out_specs=(V, V, V),
        compiler_params=SMALL, name="inner",
    )
    inner, first, lines = inner_call(
        queries, key_rows, value_rows, out_gain.reshape(1, width),
        doc_starts, doc_domains, domain_weights,
    )
    carry_call = pl.pallas_call(
        carry_kernel,
        out_shape=(
            pltpu.VMEM((blocks, rows * heads, HEAD_DIM), bf16), shape((8, LANES), f32),
        ),
        in_specs=[V, V], out_specs=(V, V),
        scratch_shapes=[pltpu.VMEM((blocks, rows * heads, HEAD_DIM), f32)],
        compiler_params=SMALL, name="carry",
    )
    carried, weight_in = carry_call(domain_weights.reshape(1, -1), states)
    carried = lax.all_to_all(carried, ("chip", "core"), 0, 0, tiled=True)
    shared = pl.pallas_call(
        attention_kernel,
        out_shape=shape((row_count + 16, width), bf16),
        in_specs=[V] * 5, out_specs=V,
        scratch_shapes=[pltpu.VMEM((HEAD_DIM, heads, HEAD_DIM), f32)],
        compiler_params=SMALL, name="attention",
    )(first, inner, carried.reshape(HEAD_DIM, heads, HEAD_DIM), lines, weight_in)
    shared = lax.all_gather(shared, "core", axis=0, tiled=False)
    side = math.isqrt(chips)
    partial, attention = pl.pallas_call(
        lambda *refs: gradient_kernel(*refs, owned=owned, side=side),
        out_shape=(
            shape((groups * width // 2, width), bf16), shape((row_count, width), bf16)
        ),
        in_specs=[V] * (1 + groups), out_specs=(V, HBM_SPEC),
        scratch_shapes=[pltpu.SemaphoreType.DMA],
        compiler_params=SMALL, name="gradient",
    )(shared, *turned)
    lines_of = [
        [[(y * side + z) * 2 + c for z in range(side)] for y in range(side)] for c in range(2)
    ]
    rows_of = [[list(line) for line in zip(*lines)] for lines in lines_of]
    partial = lax.all_to_all(
        partial.reshape(side, side * owned, width), ("chip", "core"), 0, 0, tiled=True,
        axis_index_groups=lines_of[0] + rows_of[1],
    )
    partial = pl.pallas_call(
        sum_kernel,
        out_shape=shape((side * owned, width), bf16),
        in_specs=[V], out_specs=V, compiler_params=SMALL, name="sum",
    )(partial)
    partial = lax.all_to_all(
        partial.reshape(side, owned, width), ("chip", "core"), 0, 0, tiled=True,
        axis_index_groups=rows_of[0] + lines_of[1],
    )
    new_weight, new_first, new_second = pl.pallas_call(
        update_kernel,
        out_shape=(shape((owned, width), f32),) * 3,
        in_specs=[V] * 4, out_specs=(V,) * 3, compiler_params=SMALL, name="update",
    )(partial, weight.T, moment_first.T, moment_second.T)
    return (attention, new_weight.T, new_first.T, new_second.T)


def solution(mesh):
    blocks, groups = mesh.devices.shape
    split = Mesh(mesh.devices.reshape(blocks // 2, 2, groups), ("chip", "core", "group"))
    seq, head = ("chip", "core"), "group"
    in_specs = (
        P(seq, head), P(seq, head), P(seq, head), P(head), P(seq), P(seq), P(),
        P(seq, head), P(head, seq), P(head, seq), P(head, seq),
    )
    out_specs = (P(seq, head), P(head, seq), P(head, seq), P(head, seq))
    return jax.shard_map(
        on_device, mesh=split, in_specs=in_specs, out_specs=out_specs, check_vma=False
    )
```

```python
import math

import jax
import jax.numpy as jnp
from jax import lax
from jax.experimental import pallas as pl
from jax.experimental.pallas import tpu as pltpu
from jax.sharding import Mesh, PartitionSpec as P


HEAD_DIM = 128
LANES = 128

first_debias = 0.9999734386011124
second_debias = 0.994079470779666

f32, bf16, i32 = jnp.float32, jnp.bfloat16, jnp.int32
VMEM_SPEC = pl.BlockSpec(memory_space=pltpu.VMEM)
HBM_SPEC = pl.BlockSpec(memory_space=pltpu.HBM)
SMALL = pltpu.CompilerParams(vmem_limit_bytes=12 * 1024 * 1024)
SMEM_SPEC = pl.BlockSpec(memory_space=pltpu.SMEM)


def iota(shape, dim):
    return lax.broadcasted_iota(i32, shape, dim)


def docs_along(starts_ref, shape, dim):
    positions = iota(shape, dim)
    total = jnp.zeros(shape, i32)
    for slot in range(starts_ref.shape[0]):
        total = total + (starts_ref[slot] <= positions).astype(i32)
    return total


def dot(a, b, contract):
    return lax.dot_general(a, b, (contract, ((), ())), preferred_element_type=f32)


def state_kernel(
    key_hbm, value_hbm, starts_hbm, domains_hbm, out_hbm,
    key_ref, value_ref, starts_ref, domains_ref, out_ref, arrived, left,
):
    copies = [
        pltpu.make_async_copy(source, target, arrived.at[which])
        for which, (source, target) in enumerate((
            (starts_hbm, starts_ref), (domains_hbm, domains_ref),
            (key_hbm, key_ref), (value_hbm, value_ref),
        ))
    ]
    for copy in copies:
        copy.start()
    row_count, width = key_ref.shape
    heads = width // HEAD_DIM
    saves = [
        pltpu.make_async_copy(out_ref.at[:, :, cols], out_hbm.at[:, :, cols], left.at[which])
        for which, cols in enumerate(
            pl.ds(head * HEAD_DIM, HEAD_DIM) for head in range(heads + 1)
        )
    ]
    copies[0].wait()
    copies[1].wait()
    starts = starts_ref[...]
    slots = starts.shape[1]
    started = jnp.sum((starts < row_count).astype(i32), axis=1, keepdims=True)
    last = iota((1, slots), 1) == started - 1
    last_domain = jnp.sum(jnp.where(last, domains_ref[...], 0), axis=1, keepdims=True)
    lane = iota((HEAD_DIM, LANES), 1)
    flag = (started > 0).astype(f32)
    out_ref[:, 0, width:] = jnp.where(
        lane == 0, flag, jnp.where(lane == 1, last_domain.astype(f32), 0.0)
    )
    saves[heads].start()
    positions = iota((row_count, HEAD_DIM), 0)
    docs = jnp.zeros((row_count, HEAD_DIM), i32)
    for slot in range(slots):
        docs = docs + (starts[:, slot : slot + 1] <= positions).astype(i32)
    in_tail = docs == started
    copies[2].wait()
    copies[3].wait()
    for head in range(heads):
        cols = slice(head * HEAD_DIM, (head + 1) * HEAD_DIM)
        keys = jnp.where(in_tail, key_ref[:, cols].astype(f32), 0.0).astype(bf16)
        out_ref[:, 0, cols] = dot(keys, value_ref[:, cols], ((0,), (0,)))
        saves[head].start()
    for save in saves:
        save.wait()


def carry_kernel(weights_ref, states_ref, carried_ref, weight_ref, total_ref):
    total, blocks = states_ref.shape[0], carried_ref.shape[0]
    rows, heads = total // blocks, carried_ref.shape[1] // (total // blocks)
    width = heads * HEAD_DIM
    info = states_ref[0::rows, 0, width:] if rows > 1 else states_ref[:, 0, width:]
    flag_col = info[:, 0:1]
    domain_col = info[:, 1:2]
    here = iota((blocks, blocks), 0)
    there = iota((blocks, blocks), 1)
    flag_row = jnp.sum(jnp.where(here == there, flag_col, 0.0), axis=0, keepdims=True)
    latest = jnp.max(
        jnp.where((flag_row > 0.0) & (there < here), there, -1), axis=1, keepdims=True
    )
    joined = jnp.where((there < here) & (there >= latest), 1.0, 0.0).astype(bf16)
    for row in range(rows):
        for head in range(heads):
            cols = slice(head * HEAD_DIM, (head + 1) * HEAD_DIM)
            state = states_ref[row::rows, 0, cols] if rows > 1 else states_ref[:, 0, cols]
            high = state.astype(bf16)
            rest = state - high.astype(f32)
            middle = rest.astype(bf16)
            low = (rest - middle.astype(f32)).astype(bf16)
            summed = dot(joined, high, ((1,), (0,)))
            summed = summed + dot(joined, middle, ((1,), (0,)))
            summed = summed + dot(joined, low, ((1,), (0,)))
            total_ref[:, row * heads + head, :] = summed
    carried_ref[...] = total_ref[...].astype(bf16)
    own = lax.axis_index("chip") * 2 + lax.axis_index("core")
    block_ids = iota((blocks, 1), 0)
    before = (flag_col > 0.0) & (block_ids < own)
    last_block = jnp.max(jnp.where(before, block_ids, -1), axis=0, keepdims=True)
    domain = jnp.sum(jnp.where(block_ids == last_block, domain_col, 0.0), axis=0, keepdims=True)
    slot = iota(weights_ref.shape, 1).astype(f32)
    weight = jnp.sum(
        jnp.where(slot == domain, weights_ref[...].astype(f32), 0.0), axis=1, keepdims=True
    )
    weight_ref[...] = jnp.broadcast_to(weight, weight_ref.shape)


def inner_kernel(
    query_ref, key_ref, value_ref, gain_ref, starts_ref, domains_ref, weights_ref,
    out_ref, first_ref, lines_ref,
):
    row_count, width = query_ref.shape
    square = (row_count, row_count)
    down, along = docs_along(starts_ref, square, 0), docs_along(starts_ref, square, 1)
    visible = (iota(square, 1) <= iota(square, 0)) & (down == along)
    first_doc = down[:, :HEAD_DIM] == 0
    for head in range(width // HEAD_DIM):
        cols = slice(head * HEAD_DIM, (head + 1) * HEAD_DIM)
        query = query_ref[:, cols]
        scores = dot(query, key_ref[:, cols], ((1,), (1,)))
        scores = jnp.where(visible, scores, 0.0).astype(bf16)
        out_ref[:, cols] = dot(scores, value_ref[:, cols], ((1,), (0,)))
        first_ref[:, cols] = jnp.where(first_doc, query.astype(f32), 0.0).astype(bf16)
    doc = docs_along(starts_ref, (1, row_count), 1)
    line = jnp.zeros((1, row_count), i32)
    for slot in range(starts_ref.shape[0]):
        weight = jnp.int32(0)
        for which in range(weights_ref.shape[0]):
            weight = jnp.where(domains_ref[slot] == which, weights_ref[which], weight)
        line = jnp.where(doc == slot + 1, weight, line)
    lines_ref[...] = jnp.zeros(lines_ref.shape, f32)
    lines_ref[0:1, :] = gain_ref[...]
    lines_ref[1:2, :row_count] = line.astype(f32)


def attention_kernel(
    first_ref, inner_ref, carried_ref, lines_ref, weight_in_ref, shared_ref, state_ref
):
    row_count, width = first_ref.shape
    state_ref[...] = carried_ref[...].astype(f32)
    for head in range(width // HEAD_DIM):
        cols = slice(head * HEAD_DIM, (head + 1) * HEAD_DIM)
        state = state_ref[:, head, :].astype(bf16)
        raw = inner_ref[:, cols] + dot(first_ref[:, cols], state, ((1,), (0,)))
        scale = lax.rsqrt(jnp.mean(raw * raw, axis=1, keepdims=True) + 1e-05)
        shared_ref[:row_count, cols] = (raw * scale * lines_ref[0:1, cols]).astype(bf16)
    line = lines_ref[1:2, :]
    line = jnp.where(line == 0.0, weight_in_ref[0:1, 0:1], line)
    shared_ref[row_count:, :] = jnp.broadcast_to(line, (16, width)).astype(bf16)


def turn_kernel(cotangent_ref, own_ref, other_ref, turned_ref, *, owned):
    width = cotangent_ref.shape[1]
    turned_ref[...] = cotangent_ref[...].T
    own = lax.axis_index("core")
    for core, out_ref in ((own, own_ref), (1 - own, other_ref)):
        for pair in range(width // (2 * owned)):
            start = pl.multiple_of(2 * pair * owned + core * owned, owned)
            out_ref[pair * owned : (pair + 1) * owned] = turned_ref[pl.ds(start, owned), :]


def gradient_kernel(shared_ref, *refs, owned, side):
    cotangent_refs, (out_ref, attention_ref, sent) = refs[:-3], refs[-3:]
    groups = len(cotangent_refs)
    _, cols, row_count = cotangent_refs[0].shape
    core, own_group = lax.axis_index("core"), lax.axis_index("group")
    save = pltpu.make_async_copy(shared_ref.at[core, :row_count], attention_ref, sent)
    save.start()
    for shift, cotangent_ref in enumerate(cotangent_refs):
        total = None
        for which in (core, 1 - core):
            near = 0 if total is None else 1
            weight = shared_ref[which, row_count : row_count + 1, :row_count].astype(f32)
            weighted = (cotangent_ref[near].astype(f32) * weight).astype(bf16)
            part = dot(weighted, shared_ref[which, :row_count, :], ((1,), (0,)))
            total = part if total is None else total + part
        total = total.astype(bf16)
        group = lax.rem(own_group - shift + groups, groups)
        for block in range(cols // owned):
            owner = group * (cols // owned) + block
            down, along = owner // side, lax.rem(owner, side)
            place = jnp.where(core == 0, along * side + down, owner)
            out_ref[pl.ds(pl.multiple_of(place * owned, owned), owned), :] = total[
                block * owned : (block + 1) * owned
            ]
    save.wait()


def sum_kernel(parts_ref, out_ref):
    out_ref[...] = jnp.sum(parts_ref[...].astype(f32), axis=0).astype(bf16)


def update_kernel(
    parts_ref, weight_ref, first_ref, second_ref, new_weight_ref, new_first_ref, new_second_ref
):
    gradient = jnp.sum(parts_ref[...].astype(f32), axis=0)
    weight = weight_ref[...]
    new_first = 0.9 * first_ref[...] + 0.1 * gradient
    new_second = 0.95 * second_ref[...] + 0.05 * gradient * gradient
    corrected_first = new_first / first_debias
    corrected_second = new_second / second_debias
    new_first_ref[...] = new_first
    new_second_ref[...] = new_second
    new_weight_ref[...] = weight - 0.01 * (
        corrected_first / (jnp.sqrt(corrected_second) + 1e-08) + 0.1 * weight
    )


def shape(dims, dtype):
    return jax.ShapeDtypeStruct(dims, dtype)


def on_device(
    queries, key_rows, value_rows, out_gain, doc_starts, doc_domains, domain_weights,
    cotangent, weight, moment_first, moment_second,
):
    chips, groups = lax.axis_size("chip"), lax.axis_size("group")
    blocks = 2 * chips
    row_count, width = queries.shape
    owned = weight.shape[1]
    rows, heads = HEAD_DIM // blocks, width // HEAD_DIM
    V, S = VMEM_SPEC, SMEM_SPEC

    own_half, other_half = pl.pallas_call(
        lambda *refs: turn_kernel(*refs, owned=owned),
        out_shape=(shape((width // 2, row_count), bf16),) * 2,
        in_specs=[V], out_specs=(V, V),
        scratch_shapes=[pltpu.VMEM((width, row_count), bf16)],
        compiler_params=SMALL, name="turn",
    )(cotangent)
    states = pl.pallas_call(
        state_kernel,
        out_shape=shape((HEAD_DIM, 1, width + LANES), f32),
        in_specs=[HBM_SPEC] * 4, out_specs=HBM_SPEC,
        scratch_shapes=[
            pltpu.VMEM(key_rows.shape, bf16), pltpu.VMEM(value_rows.shape, bf16),
            pltpu.VMEM((1, doc_starts.shape[0]), i32), pltpu.VMEM((1, doc_starts.shape[0]), i32),
            pltpu.VMEM((HEAD_DIM, 1, width + LANES), f32),
            pltpu.SemaphoreType.DMA((4,)), pltpu.SemaphoreType.DMA((heads + 1,)),
        ],
        compiler_params=SMALL, name="state",
    )(*(
        pltpu.with_memory_space_constraint(operand, pltpu.HBM)
        for operand in (
            key_rows, value_rows, doc_starts.reshape(1, -1), doc_domains.reshape(1, -1)
        )
    ))
    states = lax.all_to_all(states, ("chip", "core"), 0, 0, tiled=True)
    partner_half = lax.ppermute(other_half, "core", [(0, 1), (1, 0)])
    halves = jnp.stack([own_half, partner_half])
    turned = [halves]
    for k in range(1, groups):
        turned.append(lax.ppermute(halves, "group", [(g, (g + k) % groups) for g in range(groups)]))
    inner_call = pl.pallas_call(
        inner_kernel,
        out_shape=(
            shape((row_count, width), f32), shape((row_count, width), bf16), shape((8, width), f32)
        ),
        in_specs=[V, V, V, V, S, S, S], out_specs=(V, V, V),
        compiler_params=SMALL, name="inner",
    )
    inner, first, lines = inner_call(
        queries, key_rows, value_rows, out_gain.reshape(1, width),
        doc_starts, doc_domains, domain_weights,
    )
    carry_call = pl.pallas_call(
        carry_kernel,
        out_shape=(
            pltpu.VMEM((blocks, rows * heads, HEAD_DIM), bf16), shape((8, LANES), f32),
        ),
        in_specs=[V, V], out_specs=(V, V),
        scratch_shapes=[pltpu.VMEM((blocks, rows * heads, HEAD_DIM), f32)],
        compiler_params=SMALL, name="carry",
    )
    carried, weight_in = carry_call(domain_weights.reshape(1, -1), states)
    carried = lax.all_to_all(carried, ("chip", "core"), 0, 0, tiled=True)
    shared = pl.pallas_call(
        attention_kernel,
        out_shape=shape((row_count + 16, width), bf16),
        in_specs=[V] * 5, out_specs=V,
        scratch_shapes=[pltpu.VMEM((HEAD_DIM, heads, HEAD_DIM), f32)],
        compiler_params=SMALL, name="attention",
    )(first, inner, carried.reshape(HEAD_DIM, heads, HEAD_DIM), lines, weight_in)
    shared = lax.all_gather(shared, "core", axis=0, tiled=False)
    side = math.isqrt(chips)
    partial, attention = pl.pallas_call(
        lambda *refs: gradient_kernel(*refs, owned=owned, side=side),
        out_shape=(
            shape((groups * width // 2, width), bf16), shape((row_count, width), bf16)
        ),
        in_specs=[V] * (1 + groups), out_specs=(V, HBM_SPEC),
        scratch_shapes=[pltpu.SemaphoreType.DMA],
        compiler_params=SMALL, name="gradient",
    )(shared, *turned)
    lines_of = [
        [[(y * side + z) * 2 + c for z in range(side)] for y in range(side)] for c in range(2)
    ]
    rows_of = [[list(line) for line in zip(*lines)] for lines in lines_of]
    partial = lax.all_to_all(
        partial.reshape(side, side * owned, width), ("chip", "core"), 0, 0, tiled=True,
        axis_index_groups=lines_of[0] + rows_of[1],
    )
    partial = pl.pallas_call(
        sum_kernel,
        out_shape=shape((side * owned, width), bf16),
        in_specs=[V], out_specs=V, compiler_params=SMALL, name="sum",
    )(partial)
    partial = lax.all_to_all(
        partial.reshape(side, owned, width), ("chip", "core"), 0, 0, tiled=True,
        axis_index_groups=rows_of[0] + lines_of[1],
    )
    new_weight, new_first, new_second = pl.pallas_call(
        update_kernel,
        out_shape=(shape((owned, width), f32),) * 3,
        in_specs=[V] * 4, out_specs=(V,) * 3, compiler_params=SMALL, name="update",
    )(partial, weight.T, moment_first.T, moment_second.T)
    return (attention, new_weight.T, new_first.T, new_second.T)


def solution(mesh):
    blocks, groups = mesh.devices.shape
    split = Mesh(mesh.devices.reshape(blocks // 2, 2, groups), ("chip", "core", "group"))
    seq, head = ("chip", "core"), "group"
    in_specs = (
        P(seq, head), P(seq, head), P(seq, head), P(head), P(seq), P(seq), P(),
        P(seq, head), P(head, seq), P(head, seq), P(head, seq),
    )
    out_specs = (P(seq, head), P(head, seq), P(head, seq), P(head, seq))
    return jax.shard_map(
        on_device, mesh=split, in_specs=in_specs, out_specs=out_specs, check_vma=False
    )
```

```python
import math

import jax
import jax.numpy as jnp
from jax import lax
from jax.experimental import pallas as pl
from jax.experimental.pallas import tpu as pltpu
from jax.sharding import Mesh, PartitionSpec as P


HEAD_DIM = 128
LANES = 128

first_debias = 0.9999734386011124
second_debias = 0.994079470779666

f32, bf16, i32 = jnp.float32, jnp.bfloat16, jnp.int32
VMEM_SPEC = pl.BlockSpec(memory_space=pltpu.VMEM)
HBM_SPEC = pl.BlockSpec(memory_space=pltpu.HBM)
SMALL = pltpu.CompilerParams(vmem_limit_bytes=12 * 1024 * 1024)
SMEM_SPEC = pl.BlockSpec(memory_space=pltpu.SMEM)


def iota(shape, dim):
    return lax.broadcasted_iota(i32, shape, dim)


def docs_along(starts_ref, shape, dim):
    positions = iota(shape, dim)
    total = jnp.zeros(shape, i32)
    for slot in range(starts_ref.shape[0]):
        total = total + (starts_ref[slot] <= positions).astype(i32)
    return total


def dot(a, b, contract):
    return lax.dot_general(a, b, (contract, ((), ())), preferred_element_type=f32)


def state_kernel(
    key_hbm, value_hbm, starts_hbm, domains_hbm, out_hbm,
    key_ref, value_ref, starts_ref, domains_ref, out_ref, arrived, left,
):
    copies = [
        pltpu.make_async_copy(source, target, arrived.at[which])
        for which, (source, target) in enumerate((
            (starts_hbm, starts_ref), (domains_hbm, domains_ref),
            (key_hbm, key_ref), (value_hbm, value_ref),
        ))
    ]
    for copy in copies:
        copy.start()
    row_count, width = key_ref.shape
    heads = width // HEAD_DIM
    saves = [
        pltpu.make_async_copy(out_ref.at[:, :, cols], out_hbm.at[:, :, cols], left.at[which])
        for which, cols in enumerate(
            pl.ds(head * HEAD_DIM, HEAD_DIM) for head in range(heads + 1)
        )
    ]
    copies[0].wait()
    copies[1].wait()
    starts = starts_ref[...]
    slots = starts.shape[1]
    started = jnp.sum((starts < row_count).astype(i32), axis=1, keepdims=True)
    last = iota((1, slots), 1) == started - 1
    last_domain = jnp.sum(jnp.where(last, domains_ref[...], 0), axis=1, keepdims=True)
    lane = iota((HEAD_DIM, LANES), 1)
    flag = (started > 0).astype(f32)
    out_ref[:, 0, width:] = jnp.where(
        lane == 0, flag, jnp.where(lane == 1, last_domain.astype(f32), 0.0)
    )
    saves[heads].start()
    positions = iota((row_count, HEAD_DIM), 0)
    docs = jnp.zeros((row_count, HEAD_DIM), i32)
    for slot in range(slots):
        docs = docs + (starts[:, slot : slot + 1] <= positions).astype(i32)
    in_tail = docs == started
    copies[2].wait()
    copies[3].wait()
    for head in range(heads):
        cols = slice(head * HEAD_DIM, (head + 1) * HEAD_DIM)
        keys = jnp.where(in_tail, key_ref[:, cols].astype(f32), 0.0).astype(bf16)
        out_ref[:, 0, cols] = dot(keys, value_ref[:, cols], ((0,), (0,)))
        saves[head].start()
    for save in saves:
        save.wait()


def carry_kernel(weights_ref, states_ref, carried_ref, weight_ref, total_ref):
    total, blocks = states_ref.shape[0], carried_ref.shape[0]
    rows, heads = total // blocks, carried_ref.shape[1] // (total // blocks)
    width = heads * HEAD_DIM
    info = states_ref[0::rows, 0, width:] if rows > 1 else states_ref[:, 0, width:]
    flag_col = info[:, 0:1]
    domain_col = info[:, 1:2]
    here = iota((blocks, blocks), 0)
    there = iota((blocks, blocks), 1)
    flag_row = jnp.sum(jnp.where(here == there, flag_col, 0.0), axis=0, keepdims=True)
    latest = jnp.max(
        jnp.where((flag_row > 0.0) & (there < here), there, -1), axis=1, keepdims=True
    )
    joined = jnp.where((there < here) & (there >= latest), 1.0, 0.0).astype(bf16)
    for row in range(rows):
        for head in range(heads):
            cols = slice(head * HEAD_DIM, (head + 1) * HEAD_DIM)
            state = states_ref[row::rows, 0, cols] if rows > 1 else states_ref[:, 0, cols]
            high = state.astype(bf16)
            rest = state - high.astype(f32)
            middle = rest.astype(bf16)
            low = (rest - middle.astype(f32)).astype(bf16)
            parts = jnp.concatenate([high, middle, low], axis=0)
            summed = dot(jnp.concatenate([joined] * 3, axis=1), parts, ((1,), (0,)))
            total_ref[:, row * heads + head, :] = summed
    carried_ref[...] = total_ref[...].astype(bf16)
    own = lax.axis_index("chip") * 2 + lax.axis_index("core")
    block_ids = iota((blocks, 1), 0)
    before = (flag_col > 0.0) & (block_ids < own)
    last_block = jnp.max(jnp.where(before, block_ids, -1), axis=0, keepdims=True)
    domain = jnp.sum(jnp.where(block_ids == last_block, domain_col, 0.0), axis=0, keepdims=True)
    slot = iota(weights_ref.shape, 1).astype(f32)
    weight = jnp.sum(
        jnp.where(slot == domain, weights_ref[...].astype(f32), 0.0), axis=1, keepdims=True
    )
    weight_ref[...] = jnp.broadcast_to(weight, weight_ref.shape)


def inner_kernel(
    query_ref, key_ref, value_ref, gain_ref, starts_ref, domains_ref, weights_ref,
    out_ref, first_ref, lines_ref,
):
    row_count, width = query_ref.shape
    square = (row_count, row_count)
    down, along = docs_along(starts_ref, square, 0), docs_along(starts_ref, square, 1)
    visible = (iota(square, 1) <= iota(square, 0)) & (down == along)
    first_doc = down[:, :HEAD_DIM] == 0
    for head in range(width // HEAD_DIM):
        cols = slice(head * HEAD_DIM, (head + 1) * HEAD_DIM)
        query = query_ref[:, cols]
        scores = dot(query, key_ref[:, cols], ((1,), (1,)))
        scores = jnp.where(visible, scores, 0.0).astype(bf16)
        out_ref[:, cols] = dot(scores, value_ref[:, cols], ((1,), (0,)))
        first_ref[:, cols] = jnp.where(first_doc, query.astype(f32), 0.0).astype(bf16)
    doc = docs_along(starts_ref, (1, row_count), 1)
    line = jnp.zeros((1, row_count), i32)
    for slot in range(starts_ref.shape[0]):
        weight = jnp.int32(0)
        for which in range(weights_ref.shape[0]):
            weight = jnp.where(domains_ref[slot] == which, weights_ref[which], weight)
        line = jnp.where(doc == slot + 1, weight, line)
    lines_ref[...] = jnp.zeros(lines_ref.shape, f32)
    lines_ref[0:1, :] = gain_ref[...]
    lines_ref[1:2, :row_count] = line.astype(f32)


def attention_kernel(
    first_ref, inner_ref, carried_ref, lines_ref, weight_in_ref, shared_ref, state_ref
):
    row_count, width = first_ref.shape
    state_ref[...] = carried_ref[...].astype(f32)
    for head in range(width // HEAD_DIM):
        cols = slice(head * HEAD_DIM, (head + 1) * HEAD_DIM)
        state = state_ref[:, head, :].astype(bf16)
        raw = inner_ref[:, cols] + dot(first_ref[:, cols], state, ((1,), (0,)))
        scale = lax.rsqrt(jnp.mean(raw * raw, axis=1, keepdims=True) + 1e-05)
        shared_ref[:row_count, cols] = (raw * scale * lines_ref[0:1, cols]).astype(bf16)
    line = lines_ref[1:2, :]
    line = jnp.where(line == 0.0, weight_in_ref[0:1, 0:1], line)
    shared_ref[row_count:, :] = jnp.broadcast_to(line, (16, width)).astype(bf16)


def turn_kernel(cotangent_ref, own_ref, other_ref, turned_ref, *, owned):
    width = cotangent_ref.shape[1]
    turned_ref[...] = cotangent_ref[...].T
    own = lax.axis_index("core")
    for core, out_ref in ((own, own_ref), (1 - own, other_ref)):
        for pair in range(width // (2 * owned)):
            start = pl.multiple_of(2 * pair * owned + core * owned, owned)
            out_ref[pair * owned : (pair + 1) * owned] = turned_ref[pl.ds(start, owned), :]


def gradient_kernel(shared_ref, *refs, owned, side):
    cotangent_refs, (out_ref, attention_ref, sent) = refs[:-3], refs[-3:]
    groups = len(cotangent_refs)
    _, cols, row_count = cotangent_refs[0].shape
    core, own_group = lax.axis_index("core"), lax.axis_index("group")
    save = pltpu.make_async_copy(shared_ref.at[core, :row_count], attention_ref, sent)
    save.start()
    for shift, cotangent_ref in enumerate(cotangent_refs):
        total = None
        for which in (core, 1 - core):
            near = 0 if total is None else 1
            weight = shared_ref[which, row_count : row_count + 1, :row_count].astype(f32)
            weighted = (cotangent_ref[near].astype(f32) * weight).astype(bf16)
            part = dot(weighted, shared_ref[which, :row_count, :], ((1,), (0,)))
            total = part if total is None else total + part
        total = total.astype(bf16)
        group = lax.rem(own_group - shift + groups, groups)
        for block in range(cols // owned):
            owner = group * (cols // owned) + block
            down, along = owner // side, lax.rem(owner, side)
            place = jnp.where(core == 0, along * side + down, owner)
            out_ref[pl.ds(pl.multiple_of(place * owned, owned), owned), :] = total[
                block * owned : (block + 1) * owned
            ]
    save.wait()


def sum_kernel(parts_ref, out_ref):
    out_ref[...] = jnp.sum(parts_ref[...].astype(f32), axis=0).astype(bf16)


def update_kernel(
    parts_ref, weight_ref, first_ref, second_ref, new_weight_ref, new_first_ref, new_second_ref
):
    gradient = jnp.sum(parts_ref[...].astype(f32), axis=0)
    weight = weight_ref[...]
    new_first = 0.9 * first_ref[...] + 0.1 * gradient
    new_second = 0.95 * second_ref[...] + 0.05 * gradient * gradient
    corrected_first = new_first / first_debias
    corrected_second = new_second / second_debias
    new_first_ref[...] = new_first
    new_second_ref[...] = new_second
    new_weight_ref[...] = weight - 0.01 * (
        corrected_first / (jnp.sqrt(corrected_second) + 1e-08) + 0.1 * weight
    )


def shape(dims, dtype):
    return jax.ShapeDtypeStruct(dims, dtype)


def on_device(
    queries, key_rows, value_rows, out_gain, doc_starts, doc_domains, domain_weights,
    cotangent, weight, moment_first, moment_second,
):
    chips, groups = lax.axis_size("chip"), lax.axis_size("group")
    blocks = 2 * chips
    row_count, width = queries.shape
    owned = weight.shape[1]
    rows, heads = HEAD_DIM // blocks, width // HEAD_DIM
    V, S = VMEM_SPEC, SMEM_SPEC

    own_half, other_half = pl.pallas_call(
        lambda *refs: turn_kernel(*refs, owned=owned),
        out_shape=(shape((width // 2, row_count), bf16),) * 2,
        in_specs=[V], out_specs=(V, V),
        scratch_shapes=[pltpu.VMEM((width, row_count), bf16)],
        compiler_params=SMALL, name="turn",
    )(cotangent)
    states = pl.pallas_call(
        state_kernel,
        out_shape=shape((HEAD_DIM, 1, width + LANES), f32),
        in_specs=[HBM_SPEC] * 4, out_specs=HBM_SPEC,
        scratch_shapes=[
            pltpu.VMEM(key_rows.shape, bf16), pltpu.VMEM(value_rows.shape, bf16),
            pltpu.VMEM((1, doc_starts.shape[0]), i32), pltpu.VMEM((1, doc_starts.shape[0]), i32),
            pltpu.VMEM((HEAD_DIM, 1, width + LANES), f32),
            pltpu.SemaphoreType.DMA((4,)), pltpu.SemaphoreType.DMA((heads + 1,)),
        ],
        compiler_params=SMALL, name="state",
    )(*(
        pltpu.with_memory_space_constraint(operand, pltpu.HBM)
        for operand in (
            key_rows, value_rows, doc_starts.reshape(1, -1), doc_domains.reshape(1, -1)
        )
    ))
    states = lax.all_to_all(states, ("chip", "core"), 0, 0, tiled=True)
    partner_half = lax.ppermute(other_half, "core", [(0, 1), (1, 0)])
    halves = jnp.stack([own_half, partner_half])
    turned = [halves]
    for k in range(1, groups):
        turned.append(lax.ppermute(halves, "group", [(g, (g + k) % groups) for g in range(groups)]))
    inner_call = pl.pallas_call(
        inner_kernel,
        out_shape=(
            shape((row_count, width), f32), shape((row_count, width), bf16), shape((8, width), f32)
        ),
        in_specs=[V, V, V, V, S, S, S], out_specs=(V, V, V),
        compiler_params=SMALL, name="inner",
    )
    inner, first, lines = inner_call(
        queries, key_rows, value_rows, out_gain.reshape(1, width),
        doc_starts, doc_domains, domain_weights,
    )
    carry_call = pl.pallas_call(
        carry_kernel,
        out_shape=(
            pltpu.VMEM((blocks, rows * heads, HEAD_DIM), bf16), shape((8, LANES), f32),
        ),
        in_specs=[V, V], out_specs=(V, V),
        scratch_shapes=[pltpu.VMEM((blocks, rows * heads, HEAD_DIM), f32)],
        compiler_params=SMALL, name="carry",
    )
    carried, weight_in = carry_call(domain_weights.reshape(1, -1), states)
    carried = lax.all_to_all(carried, ("chip", "core"), 0, 0, tiled=True)
    shared = pl.pallas_call(
        attention_kernel,
        out_shape=shape((row_count + 16, width), bf16),
        in_specs=[V] * 5, out_specs=V,
        scratch_shapes=[pltpu.VMEM((HEAD_DIM, heads, HEAD_DIM), f32)],
        compiler_params=SMALL, name="attention",
    )(first, inner, carried.reshape(HEAD_DIM, heads, HEAD_DIM), lines, weight_in)
    shared = lax.all_gather(shared, "core", axis=0, tiled=False)
    side = math.isqrt(chips)
    partial, attention = pl.pallas_call(
        lambda *refs: gradient_kernel(*refs, owned=owned, side=side),
        out_shape=(
            shape((groups * width // 2, width), bf16), shape((row_count, width), bf16)
        ),
        in_specs=[V] * (1 + groups), out_specs=(V, HBM_SPEC),
        scratch_shapes=[pltpu.SemaphoreType.DMA],
        compiler_params=SMALL, name="gradient",
    )(shared, *turned)
    lines_of = [
        [[(y * side + z) * 2 + c for z in range(side)] for y in range(side)] for c in range(2)
    ]
    rows_of = [[list(line) for line in zip(*lines)] for lines in lines_of]
    partial = lax.all_to_all(
        partial.reshape(side, side * owned, width), ("chip", "core"), 0, 0, tiled=True,
        axis_index_groups=lines_of[0] + rows_of[1],
    )
    partial = pl.pallas_call(
        sum_kernel,
        out_shape=shape((side * owned, width), bf16),
        in_specs=[V], out_specs=V, compiler_params=SMALL, name="sum",
    )(partial)
    partial = lax.all_to_all(
        partial.reshape(side, owned, width), ("chip", "core"), 0, 0, tiled=True,
        axis_index_groups=rows_of[0] + lines_of[1],
    )
    new_weight, new_first, new_second = pl.pallas_call(
        update_kernel,
        out_shape=(shape((owned, width), f32),) * 3,
        in_specs=[V] * 4, out_specs=(V,) * 3, compiler_params=SMALL, name="update",
    )(partial, weight.T, moment_first.T, moment_second.T)
    return (attention, new_weight.T, new_first.T, new_second.T)


def solution(mesh):
    blocks, groups = mesh.devices.shape
    split = Mesh(mesh.devices.reshape(blocks // 2, 2, groups), ("chip", "core", "group"))
    seq, head = ("chip", "core"), "group"
    in_specs = (
        P(seq, head), P(seq, head), P(seq, head), P(head), P(seq), P(seq), P(),
        P(seq, head), P(head, seq), P(head, seq), P(head, seq),
    )
    out_specs = (P(seq, head), P(head, seq), P(head, seq), P(head, seq))
    return jax.shard_map(
        on_device, mesh=split, in_specs=in_specs, out_specs=out_specs, check_vma=False
    )
```
